32 devices in a mesh: ctx: 4 (over z), dp: 2 (over x), expert: 4 (over y, core).
Axes of the slice: x: 2, y: 2, z: 4, core: 2. Of those that a mesh axis runs over, the one named last changes fastest.
Arguments:
- tokens: bfloat16 [8, 1024, 2048], P(('dp', 'expert'), 'ctx'), may hold values from -6 to 6
- routes: int32 [8, 1024, 8], P(('dp', 'expert'), 'ctx'), may hold values from 0 to 15, all different within a row; in each aligned block of 256 rows (0 to 255, 256 to 511, ..., all dimensions but the last counted through in order) at most 176 rows name the same one
- w_query: bfloat16 [2048, 2048], replicated, may hold values from -0.125 to 0.125
- w_key: bfloat16 [2048, 2048], replicated, may hold values from -0.125 to 0.125
- w_value: bfloat16 [2048, 2048], replicated, may hold values from -0.125 to 0.125
- w_out: bfloat16 [2048, 2048], replicated, may hold values from -3 to 3
- attn_gain: float32 [2048], replicated, may hold values from 0.5 to 1.5
- query_gain: float32 [2048], replicated, may hold values from 0.5 to 1.5
- key_gain: float32 [2048], replicated, may hold values from 0.5 to 1.5
- mlp_gain: float32 [2048], replicated, may hold values from 0.5 to 1.5
- router: bfloat16 [2048, 16], replicated, may hold values from -0.125 to 0.125
- w_gate: bfloat16 [16, 2048, 1024], P('expert'), may hold values from -0.125 to 0.125
- w_up: bfloat16 [16, 2048, 1024], P('expert'), may hold values from -0.125 to 0.125
- w_down: bfloat16 [16, 1024, 2048], P('expert'), may hold values from -1.5 to 1.5
- cotangent: bfloat16 [8, 1024, 2048], P(('dp', 'expert'), 'ctx'), may hold values from -6 to 6
Outputs:
- mixed: bfloat16 [8, 1024, 2048], P(('dp', 'expert'), 'ctx')
- input_grad: float32 [8, 1024, 2048], P(('dp', 'expert'), 'ctx')
- grad_query: float32 [2048, 2048], P(('ctx', 'dp', 'expert'))
- grad_key: float32 [2048, 2048], P(('ctx', 'dp', 'expert'))
- grad_value: float32 [2048, 2048], P(('ctx', 'dp', 'expert'))
- grad_out: float32 [2048, 2048], P(('ctx', 'dp', 'expert'))
- grad_attn_gain: float32 [2048], P(('ctx', 'dp', 'expert'))
- grad_query_gain: float32 [2048], P(('ctx', 'dp', 'expert'))
- grad_key_gain: float32 [2048], P(('ctx', 'dp', 'expert'))
- grad_mlp_gain: float32 [2048], P(('ctx', 'dp', 'expert'))
- grad_router: float32 [2048, 16], P(('ctx', 'dp', 'expert'))
- grad_gate: float32 [16, 2048, 1024], P('expert', ('ctx', 'dp'))
- grad_up: float32 [16, 2048, 1024], P('expert', ('ctx', 'dp'))
- grad_down: float32 [16, 1024, 2048], P('expert', ('ctx', 'dp'))
The draws below stay inside these ranges and needn't reach their ends.
Inputs may be any that keep to these rules, and one draw needn't show every extreme that they name: `routes`: each row names 8 different experts. Within each device's aligned block of 256 tokens no expert is named by more than 176 tokens, and some block reaches that bound.
All inputs are finite; a program needn't handle non-finite values.
Results may differ from the reference program's by a relative error of at most 0.03.
Values may be sent and summed in bfloat16 or wider, within the bound.
No kernel may reach another device: no remote copies, remote signals or barrier semaphores. Data moves between devices by JAX's collectives and lax.ppermute only.
A program may use at most 448 MiB of HBM per device.

```python
import math
import jax
import jax.numpy as jnp
import numpy as np
from jax import lax

D = 2048
HEADS = 16
HEAD_DIM = 128
FF = 1024
TOPK = 8
TOK_DEV = 256
EXPERTS = 16
LEN = 1024
SEQS = 8
CAP = 176


def level_of(own_key, extent, shards, least, largest):
    factor_of, own = 1.0, jax.random.fold_in(own_key, 6)
    for axis_at, blocks in shards:
        steps = jnp.exp(jax.random.uniform(jax.random.fold_in(own, axis_at), (blocks,), jnp.float32, least / len(shards), largest / len(shards)))
        factor_of = factor_of * jnp.repeat(steps, extent[axis_at] // blocks).reshape([-1 if axis == axis_at else 1 for axis in range(len(extent))])
    return factor_of


def shared_out(rng, own, number, rows, number_of, top, bound, lean):
    ranking = jax.random.permutation(rng, number_of)
    heavy_load, common = load_shares(number_of, rows * top, bound, lean, True), load_shares(number_of, rows * top, bound, lean, False)
    places = jnp.arange(number_of)

    def named(sizes, rotation):
        used = int((sizes > 0).sum())
        fixed = max(1, used // 4)
        shifted = fixed + (places - fixed + rotation * (used - fixed)) % max(1, number_of - fixed)
        return jnp.zeros((number_of,), jnp.int32).at[ranking[jnp.where(places < fixed, places, shifted)]].set(jnp.asarray(sizes, jnp.int32))

    sizes = jnp.where(number % 4 == 0, named(heavy_load, number // 4), named(common, number - number // 4 - 1))
    mixed = jax.random.permutation(jax.random.fold_in(own, 3), number_of)
    donor, taker = mixed[0:number_of // 2 * 2:2], mixed[1:number_of // 2 * 2:2]
    slack = jnp.minimum(sizes[donor] - 1, bound - sizes[taker]) // 2
    slack = jnp.where((donor == ranking[0]) | (taker == ranking[0]) | (sizes[taker] == 0), 0, jnp.maximum(slack, 0))
    shifted = jax.random.randint(jax.random.fold_in(own, 4), (number_of // 2,), 0, 1 << 20) % (slack + 1)
    sizes = sizes.at[donor].add(-shifted).at[taker].add(shifted)
    labels = jnp.searchsorted(jnp.cumsum(sizes), jnp.arange(rows * top), side="right").astype(jnp.int32)
    listing = labels.reshape(top, rows).T
    listing = listing[jax.random.permutation(jax.random.fold_in(own, 1), rows)]
    rotation = jax.random.randint(jax.random.fold_in(own, 2), (rows, 1), 0, top)
    return jnp.take_along_axis(listing, (jnp.arange(top)[None, :] + rotation) % top, axis=1)


def load_shares(number_of, total, reach, slope, full):
    loads = [(1 << 20) // math.isqrt(rank ** slope) + 1 for rank in range(1, number_of + 1)]
    largest = reach if full else min(reach, max(-(-total // number_of), total * loads[0] // sum(loads)))
    least = 1 if total - largest >= number_of - 1 else 0
    given, rest = [largest] + [least] * (number_of - 1), total - largest - least * (number_of - 1)
    while rest > 0:
        candidates = [i for i in range(1, number_of) if given[i] < largest] or [i for i in range(1, number_of) if given[i] < reach]
        whole, remaining = sum([loads[i] for i in candidates]), rest
        for i in candidates:
            addition = min(reach - given[i], max(1, remaining * loads[i] // whole), rest)
            given[i] = given[i] + addition
            rest = rest - addition
    return np.array(given)


def centred(key, dims, width, most, split=(), kind=jnp.bfloat16):
    values = width * jax.random.normal(key, dims, jnp.float32)
    if split:
        values = values * level_of(key, dims, split, -0.22, 0.18)
    return jnp.clip(values, -most, most).astype(kind)


def setup_inputs(seed: int = 0) -> dict:
    seeds = jax.random.split(jax.random.key(seed), 16)
    tokens = centred(seeds[0], (SEQS, LEN, D), 1.0, 6.0, ((0, 8), (1, 4)))
    routes_keys = jax.random.split(jax.random.fold_in(seeds[1], 1), SEQS * LEN // TOK_DEV)
    routes_turns = jax.random.permutation(jax.random.fold_in(seeds[1], 3), SEQS * LEN // TOK_DEV)
    routes = jax.vmap(lambda own, number: shared_out(jax.random.fold_in(seeds[1], 2), own, number, TOK_DEV, EXPERTS, TOPK, CAP, 1))(routes_keys, routes_turns).reshape((SEQS, LEN, TOPK))
    w_query = centred(seeds[2], (D, D), D ** -0.5, 0.125)
    w_key = centred(seeds[3], (D, D), D ** -0.5, 0.125)
    w_value = centred(seeds[4], (D, D), D ** -0.5, 0.125)
    w_out = centred(seeds[5], (D, D), (max(1, 2 * D // LEN)) ** -0.5, 3.0)
    attn_gain = jnp.clip(1.0 + 0.1 * jax.random.normal(seeds[6], (D,), jnp.float32), 0.5, 1.5)
    query_gain = jnp.clip(1.0 + 0.1 * jax.random.normal(seeds[7], (D,), jnp.float32), 0.5, 1.5)
    key_gain = jnp.clip(1.0 + 0.1 * jax.random.normal(seeds[8], (D,), jnp.float32), 0.5, 1.5)
    mlp_gain = jnp.clip(1.0 + 0.1 * jax.random.normal(seeds[9], (D,), jnp.float32), 0.5, 1.5)
    router = centred(seeds[10], (D, EXPERTS), D ** -0.5, 0.125)
    w_gate = centred(seeds[11], (EXPERTS, D, FF), D ** -0.5, 0.125, ((0, 4),))
    w_up = centred(seeds[12], (EXPERTS, D, FF), D ** -0.5, 0.125, ((0, 4),))
    w_down = centred(seeds[13], (EXPERTS, FF, D), (max(1, FF // 64)) ** -0.5, 1.5, ((0, 4),))
    cotangent = centred(seeds[14], (SEQS, LEN, D), 1.0, 6.0, ((0, 8), (1, 4)))
    return dict(tokens=tokens, routes=routes, w_query=w_query, w_key=w_key, w_value=w_value, w_out=w_out, attn_gain=attn_gain, query_gain=query_gain, key_gain=key_gain, mlp_gain=mlp_gain, router=router, w_gate=w_gate, w_up=w_up, w_down=w_down, cotangent=cotangent)


EPSILON = 1e-05
HIGHEST = lax.Precision.HIGHEST

@jax.custom_vjp
def low(v):
    return lax.optimization_barrier(v.astype(jnp.bfloat16)).astype(jnp.float32)

@jax.custom_vjp
def low_back(v):
    return v

def low_keep(v):
    return (low(v), None)

def low_pass(kept, grad):
    return (grad,)

def back_keep(v):
    return (v, None)

def back_low(kept, grad):
    return (low(grad),)
low.defvjp(low_keep, low_pass)
low_back.defvjp(back_keep, back_low)

def rms_scaled(values, gain):
    return values * lax.rsqrt(lax.optimization_barrier(jnp.mean(values * values, axis=-1, keepdims=True)) + EPSILON) * gain

def rope_tables(length):
    halfway = HEAD_DIM // 2
    frequency = 10000.0 ** (-jnp.arange(halfway, dtype=jnp.float32) * 2.0 / HEAD_DIM)
    angles = jnp.arange(length, dtype=jnp.float32)[:, None] * frequency[None, :]
    angles = jnp.concatenate([angles, angles], axis=1)
    return (jnp.cos(angles), jnp.sin(angles))

def rotated(heads_rows, cosine, sine_table):
    halfway = HEAD_DIM // 2
    turned = jnp.concatenate([-heads_rows[..., halfway:], heads_rows[..., :halfway]], axis=-1)
    return heads_rows * cosine[:, None, :] + turned * sine_table[:, None, :]

def attention(queries, keys_all, values_all):
    length = queries.shape[0]
    block_rows = math.gcd(length, 512)
    block_count = length // block_rows
    score_scale = HEAD_DIM ** (-0.5)
    query_blocks = queries.reshape(block_count, block_rows, HEADS, HEAD_DIM)
    key_positions = jnp.arange(length, dtype=jnp.int32)

    def one_block(query_pair):
        query_rows, first_row = query_pair
        scores = jnp.einsum('qhd,khd->hqk', query_rows, keys_all, precision=HIGHEST) * score_scale
        scores = low_back(scores)
        query_positions = first_row + jnp.arange(block_rows, dtype=jnp.int32)
        visible = key_positions[None, :] <= query_positions[:, None]
        scores = jnp.where(visible[None], scores, -1e+30)
        weights = low(jax.nn.softmax(scores, axis=-1))
        return jnp.einsum('hqk,khd->qhd', weights, values_all, precision=HIGHEST)
    starts = jnp.arange(block_count, dtype=jnp.int32) * block_rows
    outputs = lax.map(jax.checkpoint(one_block), (query_blocks, starts))
    return outputs.reshape(length, HEADS * HEAD_DIM)

def layer_rows(params, inputs, picked):
    w_query, w_key, w_value, w_out, attn_gain, query_gain, key_gain, mlp_gain, router, w_gate, w_up, w_down = params
    length = inputs.shape[0]
    cosine, sine_table = rope_tables(length)
    normed = low(rms_scaled(inputs, attn_gain))
    query_lin = low_back(jnp.dot(normed, w_query, precision=HIGHEST))
    key_lin = low_back(jnp.dot(normed, w_key, precision=HIGHEST))
    value_rows = low(low_back(jnp.dot(normed, w_value, precision=HIGHEST)))
    queries = low(rotated(rms_scaled(query_lin, query_gain).reshape(length, HEADS, HEAD_DIM), cosine, sine_table))
    keys_all = low(rotated(rms_scaled(key_lin, key_gain).reshape(length, HEADS, HEAD_DIM), cosine, sine_table))
    attended = low_back(low(attention(queries, keys_all, value_rows.reshape(length, HEADS, HEAD_DIM))))
    hidden = inputs + low_back(jnp.dot(attended, w_out, precision=HIGHEST))
    expert_in = low(rms_scaled(hidden, mlp_gain))
    logits = low_back(jnp.dot(expert_in, router, precision=HIGHEST))
    gate_probs = jax.nn.softmax(logits, axis=-1)
    chosen = lax.optimization_barrier(jnp.sum((picked[:, :, None] == jnp.arange(EXPERTS, dtype=jnp.int32)[None, None, :]).astype(jnp.float32), axis=1))
    mixing = (gate_probs * chosen).T

    def one_expert(running, slab):
        gate_w, up_w, down_w, column = slab
        source = low_back(expert_in)
        gate_pre = low_back(jnp.dot(source, gate_w, precision=HIGHEST))
        up_pre = low_back(jnp.dot(source, up_w, precision=HIGHEST))
        activated = low(jax.nn.silu(gate_pre) * up_pre)
        result = low_back(low(jnp.dot(activated, down_w, precision=HIGHEST)))
        return (running + column[:, None] * result, None)
    expert_total, _ = lax.scan(jax.checkpoint(one_expert), jnp.zeros_like(hidden), (w_gate, w_up, w_down, mixing))
    return hidden + expert_total

def reference(tokens, routes, w_query, w_key, w_value, w_out, attn_gain, query_gain, key_gain, mlp_gain, router, w_gate, w_up, w_down, cotangent):
    params = tuple((array.astype(jnp.float32) for array in (w_query, w_key, w_value, w_out, attn_gain, query_gain, key_gain, mlp_gain, router, w_gate, w_up, w_down)))
    inputs = tokens.astype(jnp.float32)

    def forward(params, inputs):

        def one_sequence(sequence_pair):
            return layer_rows(params, sequence_pair[0], sequence_pair[1])
        return lax.map(jax.checkpoint(one_sequence), (inputs, routes))
    result, pull = jax.vjp(forward, params, inputs)
    param_grads, input_grad = pull(cotangent.astype(jnp.float32))
    return (result.astype(jnp.bfloat16), input_grad, param_grads[0], param_grads[1], param_grads[2], param_grads[3], param_grads[4], param_grads[5], param_grads[6], param_grads[7], param_grads[8], param_grads[9], param_grads[10], param_grads[11])
```

```python
import jax
import jax.numpy as jnp
from jax import lax
from jax.sharding import PartitionSpec as P

HEADS = 16
HEAD_DIM = 128


EPSILON = 1e-05
FLOAT = jnp.float32
BRAIN = jnp.bfloat16


def norm_inverse(values):
    return lax.rsqrt(jnp.mean(values * values, axis=-1, keepdims=True) + EPSILON)


def norm_backward(values, inverse, gain, upstream):
    weighted = upstream * gain
    gain_grad = jnp.sum(upstream * values * inverse, axis=0)
    value_grad = inverse * weighted - values * inverse * inverse * inverse * jnp.mean(
        weighted * values, axis=-1, keepdims=True
    )
    return (value_grad, gain_grad)


def rope_tables(positions):
    halfway = HEAD_DIM // 2
    frequency = 10000.0 ** (-jnp.arange(halfway, dtype=FLOAT) * 2.0 / HEAD_DIM)
    angles = positions.astype(FLOAT)[:, None] * frequency[None, :]
    angles = jnp.concatenate([angles, angles], axis=1)
    return (jnp.cos(angles), jnp.sin(angles))


def rotated(heads_rows, cosine, sine_table):
    halfway = HEAD_DIM // 2
    turned = jnp.concatenate([-heads_rows[..., halfway:], heads_rows[..., :halfway]], axis=-1)
    return heads_rows * cosine[:, None, :] + turned * sine_table[:, None, :]


def rotated_back(grads, cosine, sine_table):
    halfway = HEAD_DIM // 2
    sined = grads * sine_table[:, None, :]
    return grads * cosine[:, None, :] + jnp.concatenate(
        [sined[..., halfway:], -sined[..., :halfway]], axis=-1
    )


def outer_sum(left, right):
    return lax.dot_general(left, right, (((0,), (0,)), ((), ())), preferred_element_type=FLOAT)


def times_transpose(left, right):
    return lax.dot_general(left, right, (((1,), (1,)), ((), ())), preferred_element_type=FLOAT)


def times(left, right):
    return jnp.dot(left, right, preferred_element_type=FLOAT)


def shards(
    tokens,
    routes,
    w_query,
    w_key,
    w_value,
    w_out,
    attn_gain,
    query_gain,
    key_gain,
    mlp_gain,
    router,
    w_gate,
    w_up,
    w_down,
    cotangent,
):
    inputs = tokens[0].astype(FLOAT)
    rows, width = inputs.shape
    ctx_count = lax.axis_size("ctx")
    dp_count = lax.axis_size("dp")
    expert_devices = lax.axis_size("expert")
    plane = ("dp", "expert")
    plane_count = dp_count * expert_devices
    everything = ("ctx", "dp", "expert")
    local_experts = w_gate.shape[0]
    experts_all = local_experts * expert_devices
    own_experts = local_experts // dp_count
    length = rows * ctx_count
    heads = HEADS // ctx_count
    columns = heads * HEAD_DIM
    score_scale = HEAD_DIM ** (-0.5)
    ctx_at = lax.axis_index("ctx")
    dp_at = lax.axis_index("dp")
    expert_at = lax.axis_index("expert")
    first_column = ctx_at * columns

    attn_inverse = norm_inverse(inputs)
    attn_in = (inputs * attn_inverse * attn_gain).astype(BRAIN)
    all_in = lax.all_gather(attn_in, "ctx", axis=0, tiled=True)
    upstream_low = cotangent[0]
    upstream = upstream_low.astype(FLOAT)
    all_upstream = lax.all_gather(upstream_low, plane, axis=0, tiled=True)

    qkv_weights = jnp.concatenate(
        [
            lax.dynamic_slice_in_dim(weights, first_column, columns, axis=1)
            for weights in (w_query, w_key, w_value)
        ],
        axis=1,
    )
    out_weights = lax.dynamic_slice_in_dim(w_out, first_column, columns, axis=0)
    query_gain_own = lax.dynamic_slice_in_dim(query_gain, first_column, columns, axis=0)
    key_gain_own = lax.dynamic_slice_in_dim(key_gain, first_column, columns, axis=0)
    inverses = jnp.concatenate(
        [norm_inverse(times(attn_in, w_query)), norm_inverse(times(attn_in, w_key))], axis=1
    )
    all_inverses = lax.all_gather(inverses, "ctx", axis=0, tiled=True)
    query_inverse = all_inverses[:, 0:1]
    key_inverse = all_inverses[:, 1:2]
    cosine, sine_table = rope_tables(jnp.arange(length, dtype=jnp.int32))

    gate_weights, up_weights, down_weights = [
        lax.dynamic_slice_in_dim(weights, dp_at * own_experts, own_experts, axis=0)
        for weights in (w_gate, w_up, w_down)
    ]
    down_back = jnp.einsum(
        "td,efd->etf", all_upstream, down_weights, preferred_element_type=FLOAT
    )

    qkv_lin = times(all_in, qkv_weights)
    query_lin = qkv_lin[:, :columns]
    key_lin = qkv_lin[:, columns : 2 * columns]
    value_heads = qkv_lin[:, 2 * columns :].astype(BRAIN).reshape(length, heads, HEAD_DIM)
    query_heads = rotated(
        (query_lin * query_inverse * query_gain_own).reshape(length, heads, HEAD_DIM),
        cosine,
        sine_table,
    ).astype(BRAIN)
    key_heads = rotated(
        (key_lin * key_inverse * key_gain_own).reshape(length, heads, HEAD_DIM), cosine, sine_table
    ).astype(BRAIN)
    positions = jnp.arange(length, dtype=jnp.int32)
    visible = (positions[None, :] <= positions[:, None])[None]
    scores = (
        jnp.einsum("qhd,khd->hqk", query_heads, key_heads, preferred_element_type=FLOAT)
        * score_scale
    )
    scores = jnp.where(visible, scores, -1e30)
    probs = jax.nn.softmax(scores, axis=-1)
    probs_low = probs.astype(BRAIN)
    attn_wide = jnp.einsum("hqk,khd->qhd", probs_low, value_heads, preferred_element_type=FLOAT)
    attn_own = attn_wide.astype(BRAIN).reshape(length, columns)
    attn_rows = lax.all_to_all(attn_own, "ctx", split_axis=0, concat_axis=1, tiled=True)
    hidden = inputs + times(attn_rows, w_out)
    mlp_inverse = norm_inverse(hidden)
    expert_in = (hidden * mlp_inverse * mlp_gain).astype(BRAIN)
    all_expert_in = lax.all_gather(expert_in, plane, axis=0, tiled=True)
    logits = times(expert_in, router)
    gate_probs = jax.nn.softmax(logits, axis=-1)
    chosen = jnp.any(
        routes[0][:, :, None] == jnp.arange(experts_all, dtype=jnp.int32)[None, None, :], axis=1
    )
    gates = jnp.where(chosen, gate_probs, 0.0)
    all_gates = lax.all_gather(gates, plane, axis=0, tiled=True)
    first_expert = expert_at * local_experts + dp_at * own_experts
    own_gates = lax.dynamic_slice_in_dim(all_gates, first_expert, own_experts, axis=1).T[:, :, None]

    gate_pre = jnp.einsum(
        "td,edf->etf", all_expert_in, gate_weights, preferred_element_type=FLOAT
    )
    up_pre = jnp.einsum("td,edf->etf", all_expert_in, up_weights, preferred_element_type=FLOAT)
    sigmoid_gate = jax.nn.sigmoid(gate_pre)
    silu_gate = gate_pre * sigmoid_gate
    activated = silu_gate * up_pre
    weighted = (own_gates * activated).astype(BRAIN)
    own_gate_grads = jnp.sum(down_back * activated, axis=-1).T
    act_grad = own_gates * down_back
    up_grad = (act_grad * silu_gate).astype(BRAIN)
    gate_grad = (act_grad * up_pre * sigmoid_gate * (1.0 + gate_pre * (1.0 - sigmoid_gate))).astype(
        BRAIN
    )
    input_rows = (
        jnp.einsum("etf,edf->td", gate_grad, gate_weights, preferred_element_type=FLOAT)
        + jnp.einsum("etf,edf->td", up_grad, up_weights, preferred_element_type=FLOAT)
    ).astype(BRAIN)
    expert_in_grad = lax.psum_scatter(input_rows, plane, scatter_dimension=0, tiled=True).astype(
        FLOAT
    )
    produced = jnp.einsum(
        "etf,efd->td", weighted, down_weights, preferred_element_type=FLOAT
    ).astype(BRAIN)
    mixed = hidden + lax.psum_scatter(produced, plane, scatter_dimension=0, tiled=True).astype(
        FLOAT
    )
    gate_grads = lax.all_to_all(
        own_gate_grads.reshape(plane_count, rows, own_experts),
        plane,
        split_axis=0,
        concat_axis=0,
        tiled=True,
    )
    gate_grads = (
        gate_grads.reshape(dp_count, expert_devices, rows, own_experts)
        .transpose(2, 1, 0, 3)
        .reshape(rows, experts_all)
    )

    def spread(partial):
        summed = lax.psum_scatter(partial.astype(BRAIN), "ctx", scatter_dimension=1, tiled=True)
        return lax.all_to_all(summed, "dp", split_axis=1, concat_axis=0, tiled=True).astype(FLOAT)

    down_weight_grad = spread(
        jnp.einsum("etf,td->efd", weighted, all_upstream, preferred_element_type=FLOAT)
    )
    gate_weight_grad = spread(
        jnp.einsum("td,etf->edf", all_expert_in, gate_grad, preferred_element_type=FLOAT)
    )
    up_weight_grad = spread(
        jnp.einsum("td,etf->edf", all_expert_in, up_grad, preferred_element_type=FLOAT)
    )

    prob_grads = jnp.where(chosen, gate_grads, 0.0)
    logit_grads = (
        gate_probs * (prob_grads - jnp.sum(prob_grads * gate_probs, axis=-1, keepdims=True))
    ).astype(BRAIN)
    router_grad = outer_sum(expert_in, logit_grads)
    expert_in_grad = expert_in_grad + times_transpose(logit_grads, router)
    hidden_part, mlp_gain_grad = norm_backward(hidden, mlp_inverse, mlp_gain, expert_in_grad)
    hidden_grad = upstream + hidden_part
    hidden_low = hidden_grad.astype(BRAIN)
    all_hidden_low = lax.all_gather(hidden_low, "ctx", axis=0, tiled=True)
    attn_grad = times_transpose(all_hidden_low, out_weights).astype(BRAIN)
    attn_grad_heads = attn_grad.reshape(length, heads, HEAD_DIM)
    out_weight_grad = lax.psum_scatter(
        outer_sum(attn_own, all_hidden_low).astype(BRAIN), plane, scatter_dimension=0, tiled=True
    ).astype(FLOAT)
    row_delta = jnp.sum(attn_wide * attn_grad_heads.astype(FLOAT), axis=-1).T
    prob_grad = jnp.einsum(
        "qhd,khd->hqk", attn_grad_heads, value_heads, preferred_element_type=FLOAT
    )
    score_grad = (probs * (prob_grad - row_delta[..., None])).astype(BRAIN)
    query_grad = (
        jnp.einsum("hqk,khd->qhd", score_grad, key_heads, preferred_element_type=FLOAT)
        * score_scale
    )
    key_grad = (
        jnp.einsum("hqk,qhd->khd", score_grad, query_heads, preferred_element_type=FLOAT)
        * score_scale
    )
    value_low = (
        jnp.einsum("hqk,qhd->khd", probs_low, attn_grad_heads, preferred_element_type=FLOAT)
        .astype(BRAIN)
        .reshape(length, columns)
    )
    query_rot_grad = rotated_back(query_grad, cosine, sine_table).reshape(length, columns)
    key_rot_grad = rotated_back(key_grad, cosine, sine_table).reshape(length, columns)
    query_weighted = query_rot_grad * query_gain_own
    key_weighted = key_rot_grad * key_gain_own
    dots = lax.psum(
        jnp.stack(
            [jnp.sum(query_weighted * query_lin, axis=-1), jnp.sum(key_weighted * key_lin, axis=-1)]
        ),
        "ctx",
    ) * (1.0 / width)
    query_gain_grad = jnp.sum(query_rot_grad * query_lin * query_inverse, axis=0)
    key_gain_grad = jnp.sum(key_rot_grad * key_lin * key_inverse, axis=0)
    query_low = (
        query_inverse * query_weighted
        - query_lin * (query_inverse * query_inverse * query_inverse * dots[0][:, None])
    ).astype(BRAIN)
    key_low = (
        key_inverse * key_weighted
        - key_lin * (key_inverse * key_inverse * key_inverse * dots[1][:, None])
    ).astype(BRAIN)
    qkv_low = jnp.concatenate([query_low, key_low, value_low], axis=1)
    attn_in_grad = lax.psum_scatter(
        times_transpose(qkv_low, qkv_weights).astype(BRAIN), "ctx", scatter_dimension=0, tiled=True
    ).astype(FLOAT)
    qkv_weight_grad = outer_sum(all_in, qkv_low).astype(BRAIN)
    qkv_weight_grad = lax.psum_scatter(
        qkv_weight_grad.reshape(ctx_count, width // ctx_count, 3 * columns),
        plane,
        scatter_dimension=1,
        tiled=True,
    )
    qkv_weight_grad = lax.all_to_all(
        qkv_weight_grad, "ctx", split_axis=0, concat_axis=0, tiled=True
    )
    out_rows = qkv_weight_grad.shape[1]
    qkv_weight_grad = (
        qkv_weight_grad.reshape(ctx_count, out_rows, 3, columns)
        .transpose(2, 1, 0, 3)
        .reshape(3, out_rows, width)
        .astype(FLOAT)
    )
    input_part, attn_gain_grad = norm_backward(inputs, attn_inverse, attn_gain, attn_in_grad)
    input_grad = hidden_grad + input_part

    empty = jnp.zeros((width,), FLOAT)
    small = jnp.concatenate(
        [
            jnp.stack(
                [
                    attn_gain_grad,
                    lax.dynamic_update_slice_in_dim(empty, query_gain_grad, first_column, axis=0),
                    lax.dynamic_update_slice_in_dim(empty, key_gain_grad, first_column, axis=0),
                    mlp_gain_grad,
                ],
                axis=1,
            ),
            router_grad,
        ],
        axis=1,
    )
    small = lax.psum_scatter(small, everything, scatter_dimension=0, tiled=True)
    return (
        mixed.astype(BRAIN)[None],
        input_grad[None],
        qkv_weight_grad[0],
        qkv_weight_grad[1],
        qkv_weight_grad[2],
        out_weight_grad,
        small[:, 0],
        small[:, 1],
        small[:, 2],
        small[:, 3],
        small[:, 4:],
        gate_weight_grad,
        up_weight_grad,
        down_weight_grad,
    )


def solution(mesh):
    return jax.shard_map(
        shards,
        mesh=mesh,
        in_specs=(
            P(("dp", "expert"), "ctx", None),
            P(("dp", "expert"), "ctx", None),
            P(),
            P(),
            P(),
            P(),
            P(),
            P(),
            P(),
            P(),
            P(),
            P("expert", None, None),
            P("expert", None, None),
            P("expert", None, None),
            P(("dp", "expert"), "ctx", None),
        ),
        out_specs=(
            P(("dp", "expert"), "ctx", None),
            P(("dp", "expert"), "ctx", None),
            P(("ctx", "dp", "expert"), None),
            P(("ctx", "dp", "expert"), None),
            P(("ctx", "dp", "expert"), None),
            P(("ctx", "dp", "expert"), None),
            P(("ctx", "dp", "expert")),
            P(("ctx", "dp", "expert")),
            P(("ctx", "dp", "expert")),
            P(("ctx", "dp", "expert")),
            P(("ctx", "dp", "expert"), None),
            P("expert", ("ctx", "dp"), None),
            P("expert", ("ctx", "dp"), None),
            P("expert", ("ctx", "dp"), None),
        ),
        check_vma=False,
    )
```

```python
import functools

import jax
import jax.numpy as jnp
from jax import lax
from jax.experimental import pallas as pl
from jax.experimental.pallas import tpu as pltpu
from jax.sharding import PartitionSpec as P

HEADS = 16
HEAD_DIM = 128


EPSILON = 1e-05
FLOAT = jnp.float32
BRAIN = jnp.bfloat16
CTX = "ctx"
DP = "dp"
EXPERT = "expert"
OWN, FAR, NEAR, BOTH, GATES, UP_BOTH, BACK, STAGE = range(8)
NEAR_SUM, FAR_SUM, MADE, RING, SENT, HALF = range(8, 14)


def norm_inverse(values):
    return lax.rsqrt(jnp.mean(values * values, axis=-1, keepdims=True) + EPSILON)


def norm_backward(values, inverse, gain, upstream):
    weighted = upstream * gain
    gain_grad = jnp.sum(upstream * values * inverse, axis=0)
    value_grad = inverse * weighted - values * inverse * inverse * inverse * jnp.mean(
        weighted * values, axis=-1, keepdims=True
    )
    return (value_grad, gain_grad)


def rope_tables(positions):
    halfway = HEAD_DIM // 2
    frequency = 10000.0 ** (-jnp.arange(halfway, dtype=FLOAT) * 2.0 / HEAD_DIM)
    angles = positions.astype(FLOAT)[:, None] * frequency[None, :]
    angles = jnp.concatenate([angles, angles], axis=1)
    return (jnp.cos(angles), jnp.sin(angles))


def rotated(heads_rows, cosine, sine_table):
    halfway = HEAD_DIM // 2
    turned = jnp.concatenate([-heads_rows[..., halfway:], heads_rows[..., :halfway]], axis=-1)
    return heads_rows * cosine[:, None, :] + turned * sine_table[:, None, :]


def rotated_back(grads, cosine, sine_table):
    halfway = HEAD_DIM // 2
    sined = grads * sine_table[:, None, :]
    return grads * cosine[:, None, :] + jnp.concatenate(
        [sined[..., halfway:], -sined[..., :halfway]], axis=-1
    )


def outer_sum(left, right):
    return lax.dot_general(left, right, (((0,), (0,)), ((), ())), preferred_element_type=FLOAT)


def times_transpose(left, right):
    return lax.dot_general(left, right, (((1,), (1,)), ((), ())), preferred_element_type=FLOAT)


def times(left, right):
    return jnp.dot(left, right, preferred_element_type=FLOAT)


def plane_shards(
    tokens,
    routes,
    w_query,
    w_key,
    w_value,
    w_out,
    attn_gain,
    query_gain,
    key_gain,
    mlp_gain,
    router,
    w_gate,
    w_up,
    w_down,
    cotangent,
):
    inputs = tokens[0].astype(FLOAT)
    rows, width = inputs.shape
    ctx_count = lax.axis_size(CTX)
    dp_count = lax.axis_size(DP)
    expert_devices = lax.axis_size(EXPERT)
    plane = (DP, EXPERT)
    plane_count = dp_count * expert_devices
    everything = (CTX, DP, EXPERT)
    local_experts = w_gate.shape[0]
    experts_all = local_experts * expert_devices
    own_experts = local_experts // dp_count
    length = rows * ctx_count
    heads = HEADS // ctx_count
    columns = heads * HEAD_DIM
    score_scale = HEAD_DIM ** (-0.5)
    ctx_at = lax.axis_index(CTX)
    dp_at = lax.axis_index(DP)
    expert_at = lax.axis_index(EXPERT)
    first_column = ctx_at * columns

    attn_inverse = norm_inverse(inputs)
    attn_in = (inputs * attn_inverse * attn_gain).astype(BRAIN)
    all_in = lax.all_gather(attn_in, CTX, axis=0, tiled=True)
    upstream_low = cotangent[0]
    upstream = upstream_low.astype(FLOAT)
    all_upstream = lax.all_gather(upstream_low, plane, axis=0, tiled=True)

    qkv_weights = jnp.concatenate(
        [
            lax.dynamic_slice_in_dim(weights, first_column, columns, axis=1)
            for weights in (w_query, w_key, w_value)
        ],
        axis=1,
    )
    out_weights = lax.dynamic_slice_in_dim(w_out, first_column, columns, axis=0)
    query_gain_own = lax.dynamic_slice_in_dim(query_gain, first_column, columns, axis=0)
    key_gain_own = lax.dynamic_slice_in_dim(key_gain, first_column, columns, axis=0)
    inverses = jnp.concatenate(
        [norm_inverse(times(attn_in, w_query)), norm_inverse(times(attn_in, w_key))], axis=1
    )
    all_inverses = lax.all_gather(inverses, CTX, axis=0, tiled=True)
    query_inverse = all_inverses[:, 0:1]
    key_inverse = all_inverses[:, 1:2]
    cosine, sine_table = rope_tables(jnp.arange(length, dtype=jnp.int32))

    gate_weights, up_weights, down_weights = [
        lax.dynamic_slice_in_dim(weights, dp_at * own_experts, own_experts, axis=0)
        for weights in (w_gate, w_up, w_down)
    ]
    down_back = jnp.einsum(
        "td,efd->etf", all_upstream, down_weights, preferred_element_type=FLOAT
    )

    qkv_lin = times(all_in, qkv_weights)
    query_lin = qkv_lin[:, :columns]
    key_lin = qkv_lin[:, columns : 2 * columns]
    value_heads = qkv_lin[:, 2 * columns :].astype(BRAIN).reshape(length, heads, HEAD_DIM)
    query_heads = rotated(
        (query_lin * query_inverse * query_gain_own).reshape(length, heads, HEAD_DIM),
        cosine,
        sine_table,
    ).astype(BRAIN)
    key_heads = rotated(
        (key_lin * key_inverse * key_gain_own).reshape(length, heads, HEAD_DIM), cosine, sine_table
    ).astype(BRAIN)
    positions = jnp.arange(length, dtype=jnp.int32)
    visible = (positions[None, :] <= positions[:, None])[None]
    scores = (
        jnp.einsum("qhd,khd->hqk", query_heads, key_heads, preferred_element_type=FLOAT)
        * score_scale
    )
    scores = jnp.where(visible, scores, -1e30)
    probs = jax.nn.softmax(scores, axis=-1)
    probs_low = probs.astype(BRAIN)
    attn_wide = jnp.einsum("hqk,khd->qhd", probs_low, value_heads, preferred_element_type=FLOAT)
    attn_own = attn_wide.astype(BRAIN).reshape(length, columns)
    attn_rows = lax.all_to_all(attn_own, CTX, split_axis=0, concat_axis=1, tiled=True)
    hidden = inputs + times(attn_rows, w_out)
    mlp_inverse = norm_inverse(hidden)
    expert_in = (hidden * mlp_inverse * mlp_gain).astype(BRAIN)
    all_expert_in = lax.all_gather(expert_in, plane, axis=0, tiled=True)
    logits = times(expert_in, router)
    gate_probs = jax.nn.softmax(logits, axis=-1)
    chosen = jnp.any(
        routes[0][:, :, None] == jnp.arange(experts_all, dtype=jnp.int32)[None, None, :], axis=1
    )
    gates = jnp.where(chosen, gate_probs, 0.0)
    all_gates = lax.all_gather(gates, plane, axis=0, tiled=True)
    first_expert = expert_at * local_experts + dp_at * own_experts
    own_gates = lax.dynamic_slice_in_dim(all_gates, first_expert, own_experts, axis=1).T[:, :, None]

    gate_pre = jnp.einsum(
        "td,edf->etf", all_expert_in, gate_weights, preferred_element_type=FLOAT
    )
    up_pre = jnp.einsum("td,edf->etf", all_expert_in, up_weights, preferred_element_type=FLOAT)
    sigmoid_gate = jax.nn.sigmoid(gate_pre)
    silu_gate = gate_pre * sigmoid_gate
    activated = silu_gate * up_pre
    weighted = (own_gates * activated).astype(BRAIN)
    own_gate_grads = jnp.sum(down_back * activated, axis=-1).T
    act_grad = own_gates * down_back
    up_grad = (act_grad * silu_gate).astype(BRAIN)
    gate_grad = (act_grad * up_pre * sigmoid_gate * (1.0 + gate_pre * (1.0 - sigmoid_gate))).astype(
        BRAIN
    )
    input_rows = (
        jnp.einsum("etf,edf->td", gate_grad, gate_weights, preferred_element_type=FLOAT)
        + jnp.einsum("etf,edf->td", up_grad, up_weights, preferred_element_type=FLOAT)
    ).astype(BRAIN)
    expert_in_grad = lax.psum_scatter(input_rows, plane, scatter_dimension=0, tiled=True).astype(
        FLOAT
    )
    produced = jnp.einsum(
        "etf,efd->td", weighted, down_weights, preferred_element_type=FLOAT
    ).astype(BRAIN)
    mixed = hidden + lax.psum_scatter(produced, plane, scatter_dimension=0, tiled=True).astype(
        FLOAT
    )
    gate_grads = lax.all_to_all(
        own_gate_grads.reshape(plane_count, rows, own_experts),
        plane,
        split_axis=0,
        concat_axis=0,
        tiled=True,
    )
    gate_grads = (
        gate_grads.reshape(dp_count, expert_devices, rows, own_experts)
        .transpose(2, 1, 0, 3)
        .reshape(rows, experts_all)
    )

    def spread(partial):
        summed = lax.psum_scatter(partial.astype(BRAIN), CTX, scatter_dimension=1, tiled=True)
        return lax.all_to_all(summed, DP, split_axis=1, concat_axis=0, tiled=True).astype(FLOAT)

    down_weight_grad = spread(
        jnp.einsum("etf,td->efd", weighted, all_upstream, preferred_element_type=FLOAT)
    )
    gate_weight_grad = spread(
        jnp.einsum("td,etf->edf", all_expert_in, gate_grad, preferred_element_type=FLOAT)
    )
    up_weight_grad = spread(
        jnp.einsum("td,etf->edf", all_expert_in, up_grad, preferred_element_type=FLOAT)
    )

    prob_grads = jnp.where(chosen, gate_grads, 0.0)
    logit_grads = (
        gate_probs * (prob_grads - jnp.sum(prob_grads * gate_probs, axis=-1, keepdims=True))
    ).astype(BRAIN)
    router_grad = outer_sum(expert_in, logit_grads)
    expert_in_grad = expert_in_grad + times_transpose(logit_grads, router)
    hidden_part, mlp_gain_grad = norm_backward(hidden, mlp_inverse, mlp_gain, expert_in_grad)
    hidden_grad = upstream + hidden_part
    hidden_low = hidden_grad.astype(BRAIN)
    all_hidden_low = lax.all_gather(hidden_low, CTX, axis=0, tiled=True)
    attn_grad = times_transpose(all_hidden_low, out_weights).astype(BRAIN)
    attn_grad_heads = attn_grad.reshape(length, heads, HEAD_DIM)
    out_weight_grad = lax.psum_scatter(
        outer_sum(attn_own, all_hidden_low).astype(BRAIN), plane, scatter_dimension=0, tiled=True
    ).astype(FLOAT)
    row_delta = jnp.sum(attn_wide * attn_grad_heads.astype(FLOAT), axis=-1).T
    prob_grad = jnp.einsum(
        "qhd,khd->hqk", attn_grad_heads, value_heads, preferred_element_type=FLOAT
    )
    score_grad = (probs * (prob_grad - row_delta[..., None])).astype(BRAIN)
    query_grad = (
        jnp.einsum("hqk,khd->qhd", score_grad, key_heads, preferred_element_type=FLOAT)
        * score_scale
    )
    key_grad = (
        jnp.einsum("hqk,qhd->khd", score_grad, query_heads, preferred_element_type=FLOAT)
        * score_scale
    )
    value_low = (
        jnp.einsum("hqk,qhd->khd", probs_low, attn_grad_heads, preferred_element_type=FLOAT)
        .astype(BRAIN)
        .reshape(length, columns)
    )
    query_rot_grad = rotated_back(query_grad, cosine, sine_table).reshape(length, columns)
    key_rot_grad = rotated_back(key_grad, cosine, sine_table).reshape(length, columns)
    query_weighted = query_rot_grad * query_gain_own
    key_weighted = key_rot_grad * key_gain_own
    dots = lax.psum(
        jnp.stack(
            [jnp.sum(query_weighted * query_lin, axis=-1), jnp.sum(key_weighted * key_lin, axis=-1)]
        ),
        CTX,
    ) * (1.0 / width)
    query_gain_grad = jnp.sum(query_rot_grad * query_lin * query_inverse, axis=0)
    key_gain_grad = jnp.sum(key_rot_grad * key_lin * key_inverse, axis=0)
    query_low = (
        query_inverse * query_weighted
        - query_lin * (query_inverse * query_inverse * query_inverse * dots[0][:, None])
    ).astype(BRAIN)
    key_low = (
        key_inverse * key_weighted
        - key_lin * (key_inverse * key_inverse * key_inverse * dots[1][:, None])
    ).astype(BRAIN)
    qkv_low = jnp.concatenate([query_low, key_low, value_low], axis=1)
    attn_in_grad = lax.psum_scatter(
        times_transpose(qkv_low, qkv_weights).astype(BRAIN), CTX, scatter_dimension=0, tiled=True
    ).astype(FLOAT)
    qkv_weight_grad = outer_sum(all_in, qkv_low).astype(BRAIN)
    qkv_weight_grad = lax.psum_scatter(
        qkv_weight_grad.reshape(ctx_count, width // ctx_count, 3 * columns),
        plane,
        scatter_dimension=1,
        tiled=True,
    )
    qkv_weight_grad = lax.all_to_all(
        qkv_weight_grad, CTX, split_axis=0, concat_axis=0, tiled=True
    )
    out_rows = qkv_weight_grad.shape[1]
    qkv_weight_grad = (
        qkv_weight_grad.reshape(ctx_count, out_rows, 3, columns)
        .transpose(2, 1, 0, 3)
        .reshape(3, out_rows, width)
        .astype(FLOAT)
    )
    input_part, attn_gain_grad = norm_backward(inputs, attn_inverse, attn_gain, attn_in_grad)
    input_grad = hidden_grad + input_part

    empty = jnp.zeros((width,), FLOAT)
    small = jnp.concatenate(
        [
            jnp.stack(
                [
                    attn_gain_grad,
                    lax.dynamic_update_slice_in_dim(empty, query_gain_grad, first_column, axis=0),
                    lax.dynamic_update_slice_in_dim(empty, key_gain_grad, first_column, axis=0),
                    mlp_gain_grad,
                ],
                axis=1,
            ),
            router_grad,
        ],
        axis=1,
    )
    small = lax.psum_scatter(small, everything, scatter_dimension=0, tiled=True)
    return (
        mixed.astype(BRAIN)[None],
        input_grad[None],
        qkv_weight_grad[0],
        qkv_weight_grad[1],
        qkv_weight_grad[2],
        out_weight_grad,
        small[:, 0],
        small[:, 1],
        small[:, 2],
        small[:, 3],
        small[:, 4:],
        gate_weight_grad,
        up_weight_grad,
        down_weight_grad,
    )


def meet(*values):
    return lax.optimization_barrier(values)


def stage_body(
    slot,
    count,
    units,
    place,
    own,
    far,
    near,
    both,
    back,
    gates,
    weights,
    weights_back,
    *rest,
):
    row_outs = rest[-12:-8]
    gate_grads_out, rows_out, grads_out, weighted_out = rest[-8:-4]
    held, grads, in_sems, out_sem = rest[-4:]
    step = pl.program_id(0)
    rows = own.shape[0]
    whole = rows_out.at[pl.ds(slot * 4 * rows, 4 * rows), :]

    @pl.when(step == 0)
    def _():
        copies = [
            pltpu.make_async_copy(block, held.at[pl.ds(at * rows, rows), :], in_sems.at[at])
            for at, block in enumerate((own, far, near, both))
        ]
        for copy in copies:
            copy.start()
        gate_grads_out[...] = jnp.zeros_like(gate_grads_out)
        for copy in copies:
            copy.wait()
        pltpu.make_async_copy(held, whole, out_sem).start()

    @pl.when(step < count)
    def _():
        lane = lax.broadcasted_iota(jnp.int32, (rows, gates.shape[1]), 1)
        wanted = lane == place[0] + step

        def one(at, carry):
            part = pl.ds(pl.multiple_of(at * rows, rows), rows)
            pre = jnp.dot(held[part, :], weights[0], preferred_element_type=FLOAT)
            gate_pre, up_pre = pre[:, :units], pre[:, units:]
            down_back = back[part, :].astype(FLOAT)
            gate = jnp.sum(
                jnp.where(wanted, gates[part, :].astype(FLOAT), 0.0), axis=1, keepdims=True
            )
            sigmoid = jax.nn.sigmoid(gate_pre)
            silu = gate_pre * sigmoid
            activated = silu * up_pre
            weighted_out[part, :] = (gate * activated).astype(BRAIN)
            gate_grad = jnp.sum(down_back * activated, axis=1, keepdims=True)
            gate_grads_out[part, :] += jnp.where(wanted, gate_grad, 0.0)
            act_grad = gate * down_back
            gate_side = (
                act_grad * up_pre * sigmoid * (1.0 + gate_pre * (1.0 - sigmoid))
            ).astype(BRAIN)
            up_side = (act_grad * silu).astype(BRAIN)
            grads_out[part, :units] = gate_side
            grads_out[part, units:] = up_side
            first = pl.multiple_of(step * 2 * units, 2 * units)
            grads[part, pl.ds(first, units)] = gate_side
            grads[part, pl.ds(first + units, units)] = up_side
            return carry

        lax.fori_loop(0, 4, one, 0)

    @pl.when(step >= count)
    def _():
        for at in range(4):
            row_outs[at][...] = jnp.dot(
                grads[at * rows : (at + 1) * rows, :],
                weights_back[...],
                preferred_element_type=FLOAT,
            ).astype(BRAIN)

    @pl.when(step == pl.num_programs(0) - 1)
    def _():
        pltpu.make_async_copy(held, whole, out_sem).wait()


def expert_stage(slot, place, blocks, down_back, gates, weights, weights_back, buffers):
    rows, width = blocks[0].shape
    count, _, both_units = weights.shape
    units = both_units // 2
    stage_rows = 4 * rows
    tiles = 4
    tile = width // tiles
    all_rows = down_back.shape[0]
    anywhere = pl.BlockSpec(memory_space=pl.ANY)

    def first_part(step):
        return jnp.minimum(step, count - 1)

    def second_part(step):
        return jnp.maximum(step - count, 0)

    whole_specs = [
        anywhere,
        pl.BlockSpec((stage_rows, both_units), lambda i, p: (slot, first_part(i))),
        pl.BlockSpec((stage_rows, units), lambda i, p: (slot, first_part(i))),
    ]
    whole_shapes = [
        jax.ShapeDtypeStruct((all_rows, width), BRAIN),
        jax.ShapeDtypeStruct((all_rows, count * both_units), BRAIN),
        jax.ShapeDtypeStruct((all_rows, count * units), BRAIN),
    ]
    previous = () if buffers is None else tuple(buffers)
    return pl.pallas_call(
        functools.partial(stage_body, slot, count, units),
        grid_spec=pltpu.PrefetchScalarGridSpec(
            num_scalar_prefetch=1,
            grid=(count + tiles,),
            in_specs=[anywhere] * 4
            + [
                pl.BlockSpec((stage_rows, units), lambda i, p: (slot, first_part(i))),
                pl.BlockSpec((stage_rows, gates.shape[1]), lambda i, p: (0, 0)),
                pl.BlockSpec((1, width, both_units), lambda i, p: (first_part(i), 0, 0)),
                pl.BlockSpec((count * both_units, tile), lambda i, p: (0, second_part(i))),
            ]
            + [anywhere] * len(previous),
            out_specs=[pl.BlockSpec((rows, tile), lambda i, p: (0, second_part(i)))] * 4
            + [pl.BlockSpec((stage_rows, gates.shape[1]), lambda i, p: (0, 0))]
            + whole_specs,
            scratch_shapes=[
                pltpu.VMEM((stage_rows, width), BRAIN),
                pltpu.VMEM((stage_rows, count * both_units), BRAIN),
                pltpu.SemaphoreType.DMA((4,)),
                pltpu.SemaphoreType.DMA,
            ],
        ),
        out_shape=[jax.ShapeDtypeStruct((rows, width), BRAIN)] * 4
        + [jax.ShapeDtypeStruct((stage_rows, gates.shape[1]), FLOAT)]
        + whole_shapes,
        input_output_aliases={9 + at: 5 + at for at in range(len(previous))},
        compiler_params=pltpu.CompilerParams(dimension_semantics=("arbitrary",)),
        cost_estimate=pl.CostEstimate(
            flops=4 * stage_rows * width * count * both_units,
            bytes_accessed=40 << 20,
            transcendentals=stage_rows * count * units,
        ),
        name="expert_stage",
    )(place, *blocks, down_back, gates, weights, weights_back, *previous)


def back_body(count, *refs):
    blocks = refs[: 4 * count]
    weights, rows_out, back_out, held, in_sems, out_sems = refs[4 * count :]
    step = pl.program_id(0)
    rows = blocks[0].shape[0]

    def incoming(slot):
        return [
            pltpu.make_async_copy(
                blocks[4 * slot + at],
                held.at[slot % 2, pl.ds(at * rows, rows), :],
                in_sems.at[slot % 2, at],
            )
            for at in range(4)
        ]

    def outgoing(slot):
        return pltpu.make_async_copy(
            held.at[slot % 2],
            rows_out.at[pl.ds(slot * 4 * rows, 4 * rows), :],
            out_sems.at[slot % 2],
        )

    for slot in range(count):

        @pl.when(step == slot)
        def _(slot=slot):
            if slot == 0:
                for copy in incoming(0):
                    copy.start()
            if slot > 0:
                outgoing(slot - 1).wait()
            if slot + 1 < count:
                for copy in incoming(slot + 1):
                    copy.start()
            for copy in incoming(slot):
                copy.wait()
            outgoing(slot).start()

    def one(at, carry):
        part = pl.ds(pl.multiple_of(at * rows, rows), rows)
        back_out[part, :] = jnp.dot(
            held[lax.rem(step, 2), part, :], weights[...], preferred_element_type=FLOAT
        ).astype(BRAIN)
        return carry

    lax.fori_loop(0, 4, one, 0)

    @pl.when(step == count - 1)
    def _():
        outgoing(count - 1).wait()


def gathered_back(blocks, weights):
    rows, width = blocks[0].shape
    count = len(blocks) // 4
    units = weights.shape[1]
    anywhere = pl.BlockSpec(memory_space=pl.ANY)
    return pl.pallas_call(
        functools.partial(back_body, count),
        grid=(count,),
        in_specs=[anywhere] * len(blocks) + [pl.BlockSpec((width, units), lambda i: (0, 0))],
        out_specs=[anywhere, pl.BlockSpec((4 * rows, units), lambda i: (i, 0))],
        scratch_shapes=[
            pltpu.VMEM((2, 4 * rows, width), BRAIN),
            pltpu.SemaphoreType.DMA((2, 4)),
            pltpu.SemaphoreType.DMA((2,)),
        ],
        out_shape=[
            jax.ShapeDtypeStruct((4 * rows * count, width), BRAIN),
            jax.ShapeDtypeStruct((4 * rows * count, units), BRAIN),
        ],
        compiler_params=pltpu.CompilerParams(dimension_semantics=("arbitrary",)),
        cost_estimate=pl.CostEstimate(
            flops=8 * rows * count * width * units,
            bytes_accessed=48 << 20,
            transcendentals=0,
        ),
        name="gathered_back",
    )(*blocks, weights)


def swap_over(values, axis, bit):
    count = lax.axis_size(axis)
    return lax.ppermute(values, axis, [(at, at ^ bit) for at in range(count)])


def shift_over(values, axis, steps):
    count = lax.axis_size(axis)
    return lax.ppermute(values, axis, [(at, (at + steps) % count) for at in range(count)])


def axis_bits(axis):
    count = lax.axis_size(axis)
    return [1 << at for at in reversed(range(count.bit_length() - 1))]


def line_shards(
    tokens,
    routes,
    w_query,
    w_key,
    w_value,
    w_out,
    attn_gain,
    query_gain,
    key_gain,
    mlp_gain,
    router,
    w_gate,
    w_up,
    w_down,
    cotangent,
):
    inputs = tokens[0].astype(FLOAT)
    rows, width = inputs.shape
    ctx_count = lax.axis_size(CTX)
    dp_count = lax.axis_size(DP)
    expert_devices = lax.axis_size(EXPERT)
    plane = (DP, EXPERT)
    everything = (CTX, DP, EXPERT)
    device_count = ctx_count * dp_count * expert_devices
    local_experts, _, units_all = w_gate.shape
    experts_all = local_experts * expert_devices
    units = units_all // ctx_count
    hidden_units = local_experts * units
    length = rows * ctx_count
    heads = HEADS // ctx_count
    columns = heads * HEAD_DIM
    score_scale = HEAD_DIM ** (-0.5)
    ctx_at = lax.axis_index(CTX)
    dp_at = lax.axis_index(DP)
    expert_at = lax.axis_index(EXPERT)
    first_column = ctx_at * columns
    ring_places = [(ctx_at + ctx_count - slot) % ctx_count for slot in range(ctx_count)]

    attn_inverse = norm_inverse(inputs)
    attn_in = (inputs * attn_inverse * attn_gain).astype(BRAIN)
    all_in = lax.all_gather(attn_in, CTX, axis=0, tiled=True)
    inverses = jnp.concatenate(
        [norm_inverse(times(attn_in, w_query)), norm_inverse(times(attn_in, w_key))], axis=1
    )
    all_inverses = lax.all_gather(inverses, CTX, axis=0, tiled=True)
    query_inverse = all_inverses[:, 0:1]
    key_inverse = all_inverses[:, 1:2]

    qkv_weights = jnp.concatenate(
        [
            lax.dynamic_slice_in_dim(weights, first_column, columns, axis=1)
            for weights in (w_query, w_key, w_value)
        ],
        axis=1,
    )
    query_gain_own = lax.dynamic_slice_in_dim(query_gain, first_column, columns, axis=0)
    key_gain_own = lax.dynamic_slice_in_dim(key_gain, first_column, columns, axis=0)
    cosine, sine_table = rope_tables(jnp.arange(length, dtype=jnp.int32))
    gate_slice, up_slice = [
        lax.dynamic_slice_in_dim(weights, ctx_at * units, units, axis=2)
        for weights in (w_gate, w_up)
    ]
    gate_up_weights = jnp.concatenate([gate_slice, up_slice], axis=2)
    gate_up_back = gate_up_weights.transpose(0, 2, 1).reshape(2 * hidden_units, width)
    down_weights = lax.dynamic_slice_in_dim(w_down, ctx_at * units, units, axis=1).reshape(
        hidden_units, width
    )

    down_across = down_weights.T
    all_in, upstream_low, gate_up_weights, gate_up_back, down_weights, down_across, qkv_weights = (
        meet(
            all_in,
            cotangent[0],
            gate_up_weights,
            gate_up_back,
            down_weights,
            down_across,
            qkv_weights,
        )
    )
    upstream = upstream_low.astype(FLOAT)
    near, far = axis_bits(EXPERT)[::-1]
    up_own = [upstream_low]
    up_own.append(shift_over(up_own[0], CTX, 1))
    up_far = [swap_over(up_own[0], EXPERT, far)]

    qkv_lin = times(all_in, qkv_weights)
    query_lin = qkv_lin[:, :columns]
    key_lin = qkv_lin[:, columns : 2 * columns]
    value_heads = qkv_lin[:, 2 * columns :].astype(BRAIN).reshape(length, heads, HEAD_DIM)
    query_heads = rotated(
        (query_lin * query_inverse * query_gain_own).reshape(length, heads, HEAD_DIM),
        cosine,
        sine_table,
    ).astype(BRAIN)
    key_heads = rotated(
        (key_lin * key_inverse * key_gain_own).reshape(length, heads, HEAD_DIM), cosine, sine_table
    ).astype(BRAIN)
    query_heads, key_heads, up_own[1], up_far[0] = meet(
        query_heads, key_heads, up_own[1], up_far[0]
    )
    up_own.append(shift_over(up_own[1], CTX, 1))
    up_far.append(swap_over(up_own[1], EXPERT, far))
    up_near = [swap_over(up_own[0], EXPERT, near)]
    up_both = [swap_over(up_far[0], EXPERT, near)]
    positions = jnp.arange(length, dtype=jnp.int32)
    visible = (positions[None, :] <= positions[:, None])[None]
    scores = (
        jnp.einsum("qhd,khd->hqk", query_heads, key_heads, preferred_element_type=FLOAT)
        * score_scale
    )
    scores = jnp.where(visible, scores, -1e30)
    probs = jax.nn.softmax(scores, axis=-1)
    probs_low = probs.astype(BRAIN)
    attn_wide = jnp.einsum("hqk,khd->qhd", probs_low, value_heads, preferred_element_type=FLOAT)
    attn_own = attn_wide.astype(BRAIN).reshape(length, columns)
    attn_own, up_own, up_far, up_near, up_both = meet(attn_own, up_own, up_far, up_near, up_both)
    up_own.append(shift_over(up_own[2], CTX, 1))
    up_far.append(swap_over(up_own[2], EXPERT, far))
    up_near.append(swap_over(up_own[1], EXPERT, near))
    up_both.append(swap_over(up_far[1], EXPERT, near))
    attn_rows = lax.all_to_all(attn_own, CTX, split_axis=0, concat_axis=1, tiled=True)
    attn_rows, up_own, up_far, up_near, up_both = meet(
        attn_rows, up_own, up_far, up_near, up_both
    )
    up_far.append(swap_over(up_own[3], EXPERT, far))
    up_near.append(swap_over(up_own[2], EXPERT, near))
    up_near.append(swap_over(up_own[3], EXPERT, near))
    up_both.append(swap_over(up_far[2], EXPERT, near))
    hidden = inputs + times(attn_rows, w_out)
    mlp_inverse = norm_inverse(hidden)
    expert_in = (hidden * mlp_inverse * mlp_gain).astype(BRAIN)
    logits = times(expert_in, router)
    gate_probs = jax.nn.softmax(logits, axis=-1)
    chosen = jnp.any(
        routes[0][:, :, None] == jnp.arange(experts_all, dtype=jnp.int32)[None, None, :], axis=1
    )
    gates = jnp.where(chosen, gate_probs, 0.0).astype(BRAIN)
    lanes = -experts_all % 128
    def dp_parts(partial, outer, inner):
        halves = partial.reshape(outer, dp_count, inner, -1)
        return (
            lax.dynamic_index_in_dim(halves, dp_at, axis=1, keepdims=False),
            swap_over(
                lax.dynamic_index_in_dim(halves, 1 - dp_at, axis=1, keepdims=False), DP, 1
            ),
        )

    def ctx_parts(blocks):
        return [
            shift_over(
                lax.dynamic_index_in_dim(
                    blocks, (ctx_at + at) % ctx_count, axis=0, keepdims=False
                ),
                CTX,
                at,
            )
            if at
            else lax.dynamic_index_in_dim(blocks, ctx_at, axis=0, keepdims=False)
            for at in range(ctx_count)
        ]

    grad_rows = width // (ctx_count * dp_count)
    padded_gates = jnp.pad(gates, ((0, 0), (0, -experts_all % 128)))
    first_expert = expert_at * local_experts
    expert_place = jnp.full((1,), first_expert, jnp.int32)

    moved_own = [expert_in]
    moved_far, moved_near, moved_both = [], [], []
    gate_slots, stages, near_sums, far_sums, half_grads = [], [], [], [], []
    buffers = produced = sent = total = total_gate = None
    gate_half = padded_gates
    for tick in range(ctx_count + 5):
        slot = tick - 2
        fresh = {}
        if tick + 1 < ctx_count:
            fresh[OWN] = shift_over(moved_own[tick], CTX, 1)
        if tick < ctx_count:
            fresh[FAR] = swap_over(moved_own[tick], EXPERT, far)
            fresh[NEAR] = swap_over(moved_own[tick], EXPERT, near)
        if 0 <= tick - 1 < ctx_count:
            fresh[BOTH] = swap_over(moved_far[tick - 1], EXPERT, near)
        if tick == 0:
            fresh[GATES] = jnp.concatenate([gate_half, swap_over(gate_half, EXPERT, far)])
            fresh[UP_BOTH] = swap_over(up_far[3], EXPERT, near)
        if tick == 1:
            fresh[GATES] = jnp.concatenate([gate_half, swap_over(gate_half, EXPERT, near)])
            fresh[BACK] = gathered_back(
                [
                    kind[at]
                    for at in range(ctx_count)
                    for kind in (up_own, up_far, up_near, up_both)
                ],
                down_across,
            )
        if 2 <= tick < ctx_count + 1:
            fresh[GATES] = shift_over(gate_slots[-1], CTX, 1)
        if 0 <= slot < ctx_count:
            fresh[STAGE] = expert_stage(
                slot,
                expert_place,
                (moved_own[slot], moved_far[slot], moved_near[slot], moved_both[slot]),
                down_back,
                gate_slots[slot],
                gate_up_weights,
                gate_up_back,
                buffers,
            )
        if 0 <= slot - 1 < ctx_count:
            grads = stages[slot - 1]
            gate_part = grads[4].astype(BRAIN)
            fresh[NEAR_SUM] = (
                grads[0] + swap_over(grads[2], EXPERT, near),
                grads[1] + swap_over(grads[3], EXPERT, near),
                gate_part[: 2 * rows] + swap_over(gate_part[2 * rows :], EXPERT, near),
            )
        if 0 <= slot - 2 < ctx_count:
            pair = near_sums[slot - 2]
            fresh[FAR_SUM] = (
                pair[0] + swap_over(pair[1], EXPERT, far),
                pair[2][:rows] + swap_over(pair[2][rows:], EXPERT, far),
            )
        if tick == ctx_count + 2:
            total, total_gate = far_sums[1]
            all_rows, all_pre_grads, all_weighted = buffers
            fresh[MADE] = [
                [
                    times(
                        all_weighted[(4 * at + 2 * part) * rows :][: 2 * rows], down_weights
                    ).astype(BRAIN)
                    for part in (0, 1)
                ]
                for at in range(ctx_count)
            ]
        if tick >= ctx_count + 2:
            fresh[RING] = (shift_over(total, CTX, 1), shift_over(total_gate, CTX, 1))
        if tick == ctx_count + 3:
            fresh[MADE] = []
            for kept, given in produced:
                taken = swap_over(given, EXPERT, near)
                fresh[MADE].append((kept[:rows] + taken[:rows], kept[rows:] + taken[rows:]))
        if tick == ctx_count + 4:
            fresh[MADE] = [produced[1][0] + swap_over(produced[1][1], EXPERT, far), produced]
            fresh[SENT] = dp_parts(half_grads[0], ctx_count, grad_rows)
        if tick >= ctx_count + 3:
            half = tick - ctx_count - 3
            fresh[HALF] = outer_sum(
                all_rows, all_pre_grads[:, half * hidden_units :][:, :hidden_units]
            ).astype(BRAIN)
        fresh = meet(fresh)[0]
        if OWN in fresh:
            moved_own.append(fresh[OWN])
        if FAR in fresh:
            moved_far.append(fresh[FAR])
            moved_near.append(fresh[NEAR])
        if BOTH in fresh:
            moved_both.append(fresh[BOTH])
        if tick == 0:
            up_both.append(fresh[UP_BOTH])
            gate_half = fresh[GATES]
        elif GATES in fresh:
            gate_slots.append(fresh[GATES])
        if BACK in fresh:
            all_upstream, down_back = fresh[BACK]
        if STAGE in fresh:
            stages.append(fresh[STAGE][:5])
            buffers = fresh[STAGE][5:]
        if NEAR_SUM in fresh:
            near_sums.append(fresh[NEAR_SUM])
        if FAR_SUM in fresh:
            far_sums.append(fresh[FAR_SUM])
        if RING in fresh:
            following = far_sums[(tick - ctx_count) % ctx_count]
            total = fresh[RING][0] + following[0]
            total_gate = fresh[RING][1] + following[1]
        if MADE in fresh:
            produced = fresh[MADE]
        if SENT in fresh:
            first_parts = fresh[SENT]
        if HALF in fresh:
            half_grads.append(fresh[HALF])
    expert_in_grad = total.astype(FLOAT)
    gate_grads = total_gate[:, :experts_all].astype(FLOAT)
    produced_total, produced = produced

    prob_grads = jnp.where(chosen, gate_grads, 0.0)
    logit_grads = (
        gate_probs * (prob_grads - jnp.sum(prob_grads * gate_probs, axis=-1, keepdims=True))
    ).astype(BRAIN)
    router_grad = outer_sum(expert_in, logit_grads)
    expert_in_grad = expert_in_grad + times_transpose(logit_grads, router)
    hidden_part, mlp_gain_grad = norm_backward(hidden, mlp_inverse, mlp_gain, expert_in_grad)
    hidden_grad = upstream + hidden_part
    hidden_low = hidden_grad.astype(BRAIN)
    attn_grad_rows = times_transpose(hidden_low, w_out).astype(BRAIN)
    attn_grad = lax.all_to_all(
        attn_grad_rows.reshape(rows, ctx_count, columns).transpose(1, 0, 2),
        CTX,
        split_axis=0,
        concat_axis=0,
        tiled=True,
    ).reshape(length, columns)
    second_parts = dp_parts(half_grads[1], ctx_count, grad_rows)
    produced_two = produced[2][0] + swap_over(produced[2][1], EXPERT, far)
    produced_three = produced[3][0] + swap_over(produced[3][1], EXPERT, far)
    down_half = outer_sum(all_weighted, all_upstream).astype(BRAIN)
    attn_grad, produced_two, produced_three, down_half, produced, hidden_low = meet(
        attn_grad, produced_two, produced_three, down_half, produced, hidden_low
    )
    attn_grad_heads = attn_grad.reshape(length, heads, HEAD_DIM)
    out_weight_grad = outer_sum(attn_rows, hidden_low).astype(BRAIN)
    out_weight_grad = lax.psum_scatter(
        out_weight_grad.reshape(ctx_count, width // ctx_count, width),
        plane,
        scatter_dimension=1,
        tiled=True,
    )
    produced_zero = produced[0][0] + swap_over(produced[0][1], EXPERT, far)
    produced_total = shift_over(produced_total, CTX, 1) + produced_two
    first_half = ctx_parts(first_parts[0] + first_parts[1])
    row_delta = jnp.sum(attn_wide * attn_grad_heads.astype(FLOAT), axis=-1).T
    prob_grad = jnp.einsum(
        "qhd,khd->hqk", attn_grad_heads, value_heads, preferred_element_type=FLOAT
    )
    score_grad = (probs * (prob_grad - row_delta[..., None])).astype(BRAIN)
    score_grad, produced_total, second_parts = meet(score_grad, produced_total, second_parts)
    produced_total = shift_over(produced_total, CTX, 1) + produced_three
    down_parts = dp_parts(down_half, local_experts, units // dp_count)
    query_grad = (
        jnp.einsum("hqk,khd->qhd", score_grad, key_heads, preferred_element_type=FLOAT)
        * score_scale
    )
    key_grad = (
        jnp.einsum("hqk,qhd->khd", score_grad, query_heads, preferred_element_type=FLOAT)
        * score_scale
    )
    value_low = (
        jnp.einsum("hqk,qhd->khd", probs_low, attn_grad_heads, preferred_element_type=FLOAT)
        .astype(BRAIN)
        .reshape(length, columns)
    )
    query_grad, key_grad, value_low, produced_total = meet(
        query_grad, key_grad, value_low, produced_total
    )
    produced_total = shift_over(produced_total, CTX, 1) + produced_zero
    second_half = ctx_parts(second_parts[0] + second_parts[1])
    query_rot_grad = rotated_back(query_grad, cosine, sine_table).reshape(length, columns)
    key_rot_grad = rotated_back(key_grad, cosine, sine_table).reshape(length, columns)
    query_weighted = query_rot_grad * query_gain_own
    key_weighted = key_rot_grad * key_gain_own
    dots = lax.psum(
        jnp.stack(
            [jnp.sum(query_weighted * query_lin, axis=-1), jnp.sum(key_weighted * key_lin, axis=-1)]
        ),
        CTX,
    ) * (1.0 / width)
    query_gain_grad = jnp.sum(query_rot_grad * query_lin * query_inverse, axis=0)
    key_gain_grad = jnp.sum(key_rot_grad * key_lin * key_inverse, axis=0)
    query_low = (
        query_inverse * query_weighted
        - query_lin * (query_inverse * query_inverse * query_inverse * dots[0][:, None])
    ).astype(BRAIN)
    key_low = (
        key_inverse * key_weighted
        - key_lin * (key_inverse * key_inverse * key_inverse * dots[1][:, None])
    ).astype(BRAIN)
    qkv_low = jnp.concatenate([query_low, key_low, value_low], axis=1)
    qkv_low, produced_total, out_weight_grad, first_half, down_parts = meet(
        qkv_low, produced_total, out_weight_grad, first_half, down_parts
    )
    mixed = hidden + produced_total.astype(FLOAT)
    down_weight_grad = (down_parts[0] + down_parts[1]).astype(FLOAT)
    out_weight_grad = sum(
        (
            part.astype(FLOAT)
            for part in ctx_parts(out_weight_grad)
        ),
        jnp.zeros(out_weight_grad.shape[1:], FLOAT),
    )

    attn_in_parts = times_transpose(qkv_low, qkv_weights)
    attn_gain_grad = jnp.sum(attn_in_parts * all_in.astype(FLOAT), axis=0) / attn_gain
    attn_in_low = attn_in_parts.astype(BRAIN)
    attn_in_slots = [
        lax.dynamic_slice_in_dim(attn_in_low, place * rows, rows, axis=0) for place in ring_places
    ]
    attn_in_total, second_half = meet(shift_over(attn_in_slots[1], CTX, 1), second_half)
    attn_in_total = attn_in_total + attn_in_slots[2]
    attn_in_total = shift_over(attn_in_total, CTX, 1) + attn_in_slots[3]
    attn_in_grad = (shift_over(attn_in_total, CTX, 1) + attn_in_slots[0]).astype(FLOAT)
    def placed(parts):
        whole = jnp.zeros((ctx_count,) + parts[0].shape, BRAIN)
        for at, part in enumerate(parts):
            whole = lax.dynamic_update_index_in_dim(whole, part, ring_places[at], axis=0)
        return whole.reshape(ctx_count, grad_rows, local_experts // 2, 2, units)

    halves = jnp.stack([placed(first_half), placed(second_half)])
    gate_weight_grad, up_weight_grad = [
        halves[:, :, :, :, side]
        .transpose(0, 3, 2, 1, 4)
        .reshape(local_experts, grad_rows, units_all)
        .astype(FLOAT)
        for side in (0, 1)
    ]
    empty = jnp.zeros((width,), FLOAT)
    small = jnp.concatenate(
        [
            jnp.stack(
                [
                    attn_gain_grad,
                    lax.dynamic_update_slice_in_dim(empty, query_gain_grad, first_column, axis=0),
                    lax.dynamic_update_slice_in_dim(empty, key_gain_grad, first_column, axis=0),
                    mlp_gain_grad,
                ],
                axis=0,
            ),
            router_grad.T,
        ],
        axis=0,
    )
    own_width = width // device_count
    small_count = 4 + experts_all
    small = small.reshape(small_count, device_count, own_width).transpose(1, 0, 2)
    small = small.reshape(ctx_count, dp_count, 2, 2, small_count * own_width // 128, 128)
    for axis, bit, mine, place in (
        (DP, 1, dp_at, 1),
        (EXPERT, far, expert_at // 2, 1),
        (EXPERT, near, expert_at % 2, 1),
    ):
        kept = lax.dynamic_index_in_dim(small, mine, axis=place, keepdims=False)
        given = lax.dynamic_index_in_dim(small, 1 - mine, axis=place, keepdims=False)
        small = kept + swap_over(given, axis, bit)
    small = sum(ctx_parts(small)).reshape(small_count, own_width)
    qkv_weight_grad = outer_sum(all_in, qkv_low).astype(BRAIN)
    qkv_weight_grad = lax.psum_scatter(
        qkv_weight_grad.reshape(ctx_count, width // ctx_count, 3 * columns),
        plane,
        scatter_dimension=1,
        tiled=True,
    )
    qkv_weight_grad = lax.all_to_all(qkv_weight_grad, CTX, split_axis=0, concat_axis=0, tiled=True)
    qkv_weight_grad = (
        qkv_weight_grad.reshape(ctx_count, own_width, 3, columns)
        .transpose(2, 1, 0, 3)
        .reshape(3, own_width, width)
        .astype(FLOAT)
    )
    input_part, _ = norm_backward(inputs, attn_inverse, attn_gain, attn_in_grad)
    input_grad = hidden_grad + input_part

    return (
        mixed.astype(BRAIN)[None],
        input_grad[None],
        qkv_weight_grad[0],
        qkv_weight_grad[1],
        qkv_weight_grad[2],
        out_weight_grad,
        small[0],
        small[1],
        small[2],
        small[3],
        small[4:].T,
        gate_weight_grad,
        up_weight_grad,
        down_weight_grad,
    )


def solution(mesh):
    sizes = mesh.shape
    small = sizes[CTX] == 4 and sizes[EXPERT] == 4 and sizes[DP] == 2
    shards = line_shards if small else plane_shards
    return jax.shard_map(
        shards,
        mesh=mesh,
        in_specs=(
            P((DP, EXPERT), CTX, None),
            P((DP, EXPERT), CTX, None),
            P(),
            P(),
            P(),
            P(),
            P(),
            P(),
            P(),
            P(),
            P(),
            P(EXPERT, None, None),
            P(EXPERT, None, None),
            P(EXPERT, None, None),
            P((DP, EXPERT), CTX, None),
        ),
        out_specs=(
            P((DP, EXPERT), CTX, None),
            P((DP, EXPERT), CTX, None),
            P((CTX, DP, EXPERT), None),
            P((CTX, DP, EXPERT), None),
            P((CTX, DP, EXPERT), None),
            P((CTX, DP, EXPERT), None),
            P((CTX, DP, EXPERT)),
            P((CTX, DP, EXPERT)),
            P((CTX, DP, EXPERT)),
            P((CTX, DP, EXPERT)),
            P((CTX, DP, EXPERT), None),
            P(EXPERT, (CTX, DP), None),
            P(EXPERT, (CTX, DP), None),
            P(EXPERT, (CTX, DP), None),
        ),
        check_vma=False,
    )
```

```python
import functools

import jax
import jax.numpy as jnp
from jax import lax
from jax.experimental import pallas as pl
from jax.experimental.pallas import tpu as pltpu
from jax.sharding import PartitionSpec as P


HEADS = 16
HEAD_DIM = 128


EPSILON = 1e-05
FLOAT = jnp.float32
BRAIN = jnp.bfloat16
CTX = "ctx"
DP = "dp"
EXPERT = "expert"
OWN, FAR, NEAR, BOTH, GATES, UP_BOTH, BACK, STAGE = range(8)
NEAR_SUM, FAR_SUM, MADE, RING, HALF = range(8, 13)


def norm_inverse(values):
    return lax.rsqrt(jnp.mean(values * values, axis=-1, keepdims=True) + EPSILON)


def norm_backward(values, inverse, gain, upstream):
    weighted = upstream * gain
    gain_grad = jnp.sum(upstream * values * inverse, axis=0)
    value_grad = inverse * weighted - values * inverse * inverse * inverse * jnp.mean(
        weighted * values, axis=-1, keepdims=True
    )
    return (value_grad, gain_grad)


def rope_tables(positions):
    halfway = HEAD_DIM // 2
    frequency = 10000.0 ** (-jnp.arange(halfway, dtype=FLOAT) * 2.0 / HEAD_DIM)
    angles = positions.astype(FLOAT)[:, None] * frequency[None, :]
    angles = jnp.concatenate([angles, angles], axis=1)
    return (jnp.cos(angles), jnp.sin(angles))


def rotated(heads_rows, cosine, sine_table):
    halfway = HEAD_DIM // 2
    turned = jnp.concatenate([-heads_rows[..., halfway:], heads_rows[..., :halfway]], axis=-1)
    return heads_rows * cosine[:, None, :] + turned * sine_table[:, None, :]


def rotated_back(grads, cosine, sine_table):
    halfway = HEAD_DIM // 2
    sined = grads * sine_table[:, None, :]
    return grads * cosine[:, None, :] + jnp.concatenate(
        [sined[..., halfway:], -sined[..., :halfway]], axis=-1
    )


def outer_sum(left, right):
    return lax.dot_general(left, right, (((0,), (0,)), ((), ())), preferred_element_type=FLOAT)


def times_transpose(left, right):
    return lax.dot_general(left, right, (((1,), (1,)), ((), ())), preferred_element_type=FLOAT)


def times(left, right):
    return jnp.dot(left, right, preferred_element_type=FLOAT)


def plane_shards(
    tokens,
    routes,
    w_query,
    w_key,
    w_value,
    w_out,
    attn_gain,
    query_gain,
    key_gain,
    mlp_gain,
    router,
    w_gate,
    w_up,
    w_down,
    cotangent,
):
    inputs = tokens[0].astype(FLOAT)
    rows, width = inputs.shape
    ctx_count = lax.axis_size(CTX)
    dp_count = lax.axis_size(DP)
    expert_devices = lax.axis_size(EXPERT)
    plane = (DP, EXPERT)
    plane_count = dp_count * expert_devices
    everything = (CTX, DP, EXPERT)
    local_experts = w_gate.shape[0]
    experts_all = local_experts * expert_devices
    own_experts = local_experts // dp_count
    length = rows * ctx_count
    heads = HEADS // ctx_count
    columns = heads * HEAD_DIM
    score_scale = HEAD_DIM ** (-0.5)
    ctx_at = lax.axis_index(CTX)
    dp_at = lax.axis_index(DP)
    expert_at = lax.axis_index(EXPERT)
    first_column = ctx_at * columns

    attn_inverse = norm_inverse(inputs)
    attn_in = (inputs * attn_inverse * attn_gain).astype(BRAIN)
    all_in = lax.all_gather(attn_in, CTX, axis=0, tiled=True)
    upstream_low = cotangent[0]
    upstream = upstream_low.astype(FLOAT)
    all_upstream = lax.all_gather(upstream_low, plane, axis=0, tiled=True)

    qkv_weights = jnp.concatenate(
        [
            lax.dynamic_slice_in_dim(weights, first_column, columns, axis=1)
            for weights in (w_query, w_key, w_value)
        ],
        axis=1,
    )
    out_weights = lax.dynamic_slice_in_dim(w_out, first_column, columns, axis=0)
    query_gain_own = lax.dynamic_slice_in_dim(query_gain, first_column, columns, axis=0)
    key_gain_own = lax.dynamic_slice_in_dim(key_gain, first_column, columns, axis=0)
    inverses = jnp.concatenate(
        [norm_inverse(times(attn_in, w_query)), norm_inverse(times(attn_in, w_key))], axis=1
    )
    all_inverses = lax.all_gather(inverses, CTX, axis=0, tiled=True)
    query_inverse = all_inverses[:, 0:1]
    key_inverse = all_inverses[:, 1:2]
    cosine, sine_table = rope_tables(jnp.arange(length, dtype=jnp.int32))

    gate_weights, up_weights, down_weights = [
        lax.dynamic_slice_in_dim(weights, dp_at * own_experts, own_experts, axis=0)
        for weights in (w_gate, w_up, w_down)
    ]
    down_back = jnp.einsum(
        "td,efd->etf", all_upstream, down_weights, preferred_element_type=FLOAT
    )

    qkv_lin = times(all_in, qkv_weights)
    query_lin = qkv_lin[:, :columns]
    key_lin = qkv_lin[:, columns : 2 * columns]
    value_heads = qkv_lin[:, 2 * columns :].astype(BRAIN).reshape(length, heads, HEAD_DIM)
    query_heads = rotated(
        (query_lin * query_inverse * query_gain_own).reshape(length, heads, HEAD_DIM),
        cosine,
        sine_table,
    ).astype(BRAIN)
    key_heads = rotated(
        (key_lin * key_inverse * key_gain_own).reshape(length, heads, HEAD_DIM), cosine, sine_table
    ).astype(BRAIN)
    positions = jnp.arange(length, dtype=jnp.int32)
    visible = (positions[None, :] <= positions[:, None])[None]
    scores = (
        jnp.einsum("qhd,khd->hqk", query_heads, key_heads, preferred_element_type=FLOAT)
        * score_scale
    )
    scores = jnp.where(visible, scores, -1e30)
    probs = jax.nn.softmax(scores, axis=-1)
    probs_low = probs.astype(BRAIN)
    attn_wide = jnp.einsum("hqk,khd->qhd", probs_low, value_heads, preferred_element_type=FLOAT)
    attn_own = attn_wide.astype(BRAIN).reshape(length, columns)
    attn_rows = lax.all_to_all(attn_own, CTX, split_axis=0, concat_axis=1, tiled=True)
    hidden = inputs + times(attn_rows, w_out)
    mlp_inverse = norm_inverse(hidden)
    expert_in = (hidden * mlp_inverse * mlp_gain).astype(BRAIN)
    all_expert_in = lax.all_gather(expert_in, plane, axis=0, tiled=True)
    logits = times(expert_in, router)
    gate_probs = jax.nn.softmax(logits, axis=-1)
    chosen = jnp.any(
        routes[0][:, :, None] == jnp.arange(experts_all, dtype=jnp.int32)[None, None, :], axis=1
    )
    gates = jnp.where(chosen, gate_probs, 0.0)
    all_gates = lax.all_gather(gates, plane, axis=0, tiled=True)
    first_expert = expert_at * local_experts + dp_at * own_experts
    own_gates = lax.dynamic_slice_in_dim(all_gates, first_expert, own_experts, axis=1).T[:, :, None]

    gate_pre = jnp.einsum(
        "td,edf->etf", all_expert_in, gate_weights, preferred_element_type=FLOAT
    )
    up_pre = jnp.einsum("td,edf->etf", all_expert_in, up_weights, preferred_element_type=FLOAT)
    sigmoid_gate = jax.nn.sigmoid(gate_pre)
    silu_gate = gate_pre * sigmoid_gate
    activated = silu_gate * up_pre
    weighted = (own_gates * activated).astype(BRAIN)
    own_gate_grads = jnp.sum(down_back * activated, axis=-1).T
    act_grad = own_gates * down_back
    up_grad = (act_grad * silu_gate).astype(BRAIN)
    gate_grad = (act_grad * up_pre * sigmoid_gate * (1.0 + gate_pre * (1.0 - sigmoid_gate))).astype(
        BRAIN
    )
    input_rows = (
        jnp.einsum("etf,edf->td", gate_grad, gate_weights, preferred_element_type=FLOAT)
        + jnp.einsum("etf,edf->td", up_grad, up_weights, preferred_element_type=FLOAT)
    ).astype(BRAIN)
    expert_in_grad = lax.psum_scatter(input_rows, plane, scatter_dimension=0, tiled=True).astype(
        FLOAT
    )
    produced = jnp.einsum(
        "etf,efd->td", weighted, down_weights, preferred_element_type=FLOAT
    ).astype(BRAIN)
    mixed = hidden + lax.psum_scatter(produced, plane, scatter_dimension=0, tiled=True).astype(
        FLOAT
    )
    gate_grads = lax.all_to_all(
        own_gate_grads.reshape(plane_count, rows, own_experts),
        plane,
        split_axis=0,
        concat_axis=0,
        tiled=True,
    )
    gate_grads = (
        gate_grads.reshape(dp_count, expert_devices, rows, own_experts)
        .transpose(2, 1, 0, 3)
        .reshape(rows, experts_all)
    )

    def spread(partial):
        summed = lax.psum_scatter(partial.astype(BRAIN), CTX, scatter_dimension=1, tiled=True)
        return lax.all_to_all(summed, DP, split_axis=1, concat_axis=0, tiled=True).astype(FLOAT)

    down_weight_grad = spread(
        jnp.einsum("etf,td->efd", weighted, all_upstream, preferred_element_type=FLOAT)
    )
    gate_weight_grad = spread(
        jnp.einsum("td,etf->edf", all_expert_in, gate_grad, preferred_element_type=FLOAT)
    )
    up_weight_grad = spread(
        jnp.einsum("td,etf->edf", all_expert_in, up_grad, preferred_element_type=FLOAT)
    )

    prob_grads = jnp.where(chosen, gate_grads, 0.0)
    logit_grads = (
        gate_probs * (prob_grads - jnp.sum(prob_grads * gate_probs, axis=-1, keepdims=True))
    ).astype(BRAIN)
    router_grad = outer_sum(expert_in, logit_grads)
    expert_in_grad = expert_in_grad + times_transpose(logit_grads, router)
    hidden_part, mlp_gain_grad = norm_backward(hidden, mlp_inverse, mlp_gain, expert_in_grad)
    hidden_grad = upstream + hidden_part
    hidden_low = hidden_grad.astype(BRAIN)
    all_hidden_low = lax.all_gather(hidden_low, CTX, axis=0, tiled=True)
    attn_grad = times_transpose(all_hidden_low, out_weights).astype(BRAIN)
    attn_grad_heads = attn_grad.reshape(length, heads, HEAD_DIM)
    out_weight_grad = lax.psum_scatter(
        outer_sum(attn_own, all_hidden_low).astype(BRAIN), plane, scatter_dimension=0, tiled=True
    ).astype(FLOAT)
    row_delta = jnp.sum(attn_wide * attn_grad_heads.astype(FLOAT), axis=-1).T
    prob_grad = jnp.einsum(
        "qhd,khd->hqk", attn_grad_heads, value_heads, preferred_element_type=FLOAT
    )
    score_grad = (probs * (prob_grad - row_delta[..., None])).astype(BRAIN)
    query_grad = (
        jnp.einsum("hqk,khd->qhd", score_grad, key_heads, preferred_element_type=FLOAT)
        * score_scale
    )
    key_grad = (
        jnp.einsum("hqk,qhd->khd", score_grad, query_heads, preferred_element_type=FLOAT)
        * score_scale
    )
    value_low = (
        jnp.einsum("hqk,qhd->khd", probs_low, attn_grad_heads, preferred_element_type=FLOAT)
        .astype(BRAIN)
        .reshape(length, columns)
    )
    query_rot_grad = rotated_back(query_grad, cosine, sine_table).reshape(length, columns)
    key_rot_grad = rotated_back(key_grad, cosine, sine_table).reshape(length, columns)
    query_weighted = query_rot_grad * query_gain_own
    key_weighted = key_rot_grad * key_gain_own
    dots = lax.psum(
        jnp.stack(
            [jnp.sum(query_weighted * query_lin, axis=-1), jnp.sum(key_weighted * key_lin, axis=-1)]
        ),
        CTX,
    ) * (1.0 / width)
    query_gain_grad = jnp.sum(query_rot_grad * query_lin * query_inverse, axis=0)
    key_gain_grad = jnp.sum(key_rot_grad * key_lin * key_inverse, axis=0)
    query_low = (
        query_inverse * query_weighted
        - query_lin * (query_inverse * query_inverse * query_inverse * dots[0][:, None])
    ).astype(BRAIN)
    key_low = (
        key_inverse * key_weighted
        - key_lin * (key_inverse * key_inverse * key_inverse * dots[1][:, None])
    ).astype(BRAIN)
    qkv_low = jnp.concatenate([query_low, key_low, value_low], axis=1)
    attn_in_grad = lax.psum_scatter(
        times_transpose(qkv_low, qkv_weights).astype(BRAIN), CTX, scatter_dimension=0, tiled=True
    ).astype(FLOAT)
    qkv_weight_grad = outer_sum(all_in, qkv_low).astype(BRAIN)
    qkv_weight_grad = lax.psum_scatter(
        qkv_weight_grad.reshape(ctx_count, width // ctx_count, 3 * columns),
        plane,
        scatter_dimension=1,
        tiled=True,
    )
    qkv_weight_grad = lax.all_to_all(
        qkv_weight_grad, CTX, split_axis=0, concat_axis=0, tiled=True
    )
    out_rows = qkv_weight_grad.shape[1]
    qkv_weight_grad = (
        qkv_weight_grad.reshape(ctx_count, out_rows, 3, columns)
        .transpose(2, 1, 0, 3)
        .reshape(3, out_rows, width)
        .astype(FLOAT)
    )
    input_part, attn_gain_grad = norm_backward(inputs, attn_inverse, attn_gain, attn_in_grad)
    input_grad = hidden_grad + input_part

    empty = jnp.zeros((width,), FLOAT)
    small = jnp.concatenate(
        [
            jnp.stack(
                [
                    attn_gain_grad,
                    lax.dynamic_update_slice_in_dim(empty, query_gain_grad, first_column, axis=0),
                    lax.dynamic_update_slice_in_dim(empty, key_gain_grad, first_column, axis=0),
                    mlp_gain_grad,
                ],
                axis=1,
            ),
            router_grad,
        ],
        axis=1,
    )
    small = lax.psum_scatter(small, everything, scatter_dimension=0, tiled=True)
    return (
        mixed.astype(BRAIN)[None],
        input_grad[None],
        qkv_weight_grad[0],
        qkv_weight_grad[1],
        qkv_weight_grad[2],
        out_weight_grad,
        small[:, 0],
        small[:, 1],
        small[:, 2],
        small[:, 3],
        small[:, 4:],
        gate_weight_grad,
        up_weight_grad,
        down_weight_grad,
    )


def meet(*values):
    return lax.optimization_barrier(values)


def stage_body(
    slot,
    count,
    units,
    place,
    own,
    far,
    near,
    both,
    back,
    gates,
    weights,
    weights_back,
    *rest,
):
    row_outs = rest[-12:-8]
    gate_grads_out, rows_out, grads_out, weighted_out = rest[-8:-4]
    held, grads, in_sems, out_sem = rest[-4:]
    step = pl.program_id(0)
    rows = own.shape[0]
    whole = rows_out.at[pl.ds(slot * 4 * rows, 4 * rows), :]

    @pl.when(step == 0)
    def _():
        copies = [
            pltpu.make_async_copy(block, held.at[pl.ds(at * rows, rows), :], in_sems.at[at])
            for at, block in enumerate((own, far, near, both))
        ]
        for copy in copies:
            copy.start()
        gate_grads_out[...] = jnp.zeros_like(gate_grads_out)
        for copy in copies:
            copy.wait()
        pltpu.make_async_copy(held, whole, out_sem).start()

    @pl.when(step < count)
    def _():
        lane = lax.broadcasted_iota(jnp.int32, (rows, gates.shape[1]), 1)
        wanted = lane == place[0] + step

        def one(at, carry):
            part = pl.ds(pl.multiple_of(at * rows, rows), rows)
            pre = jnp.dot(held[part, :], weights[0], preferred_element_type=FLOAT)
            gate_pre, up_pre = pre[:, :units], pre[:, units:]
            down_back = back[part, :].astype(FLOAT)
            gate = jnp.sum(
                jnp.where(wanted, gates[part, :].astype(FLOAT), 0.0), axis=1, keepdims=True
            )
            sigmoid = jax.nn.sigmoid(gate_pre)
            silu = gate_pre * sigmoid
            activated = silu * up_pre
            weighted_out[part, :] = (gate * activated).astype(BRAIN)
            gate_grad = jnp.sum(down_back * activated, axis=1, keepdims=True)
            gate_grads_out[part, :] += jnp.where(wanted, gate_grad, 0.0)
            act_grad = gate * down_back
            gate_side = (
                act_grad * up_pre * sigmoid * (1.0 + gate_pre * (1.0 - sigmoid))
            ).astype(BRAIN)
            up_side = (act_grad * silu).astype(BRAIN)
            grads_out[part, :units] = gate_side
            grads_out[part, units:] = up_side
            first = pl.multiple_of(step * 2 * units, 2 * units)
            grads[part, pl.ds(first, units)] = gate_side
            grads[part, pl.ds(first + units, units)] = up_side
            return carry

        lax.fori_loop(0, 4, one, 0, unroll=4)

    @pl.when(step >= count)
    def _():
        for at in range(4):
            row_outs[at][...] = jnp.dot(
                grads[at * rows : (at + 1) * rows, :],
                weights_back[...],
                preferred_element_type=FLOAT,
            ).astype(BRAIN)

    @pl.when(step == pl.num_programs(0) - 1)
    def _():
        pltpu.make_async_copy(held, whole, out_sem).wait()


def expert_stage(slot, place, blocks, down_back, gates, weights, weights_back, buffers):
    rows, width = blocks[0].shape
    count, _, both_units = weights.shape
    units = both_units // 2
    stage_rows = 4 * rows
    tiles = 4
    tile = width // tiles
    all_rows = down_back.shape[0]
    anywhere = pl.BlockSpec(memory_space=pl.ANY)

    def first_part(step):
        return jnp.minimum(step, count - 1)

    def second_part(step):
        return jnp.maximum(step - count, 0)

    whole_specs = [
        anywhere,
        pl.BlockSpec((stage_rows, both_units), lambda i, p: (slot, first_part(i))),
        pl.BlockSpec((stage_rows, units), lambda i, p: (slot, first_part(i))),
    ]
    whole_shapes = [
        jax.ShapeDtypeStruct((all_rows, width), BRAIN),
        jax.ShapeDtypeStruct((all_rows, count * both_units), BRAIN),
        jax.ShapeDtypeStruct((all_rows, count * units), BRAIN),
    ]
    previous = () if buffers is None else tuple(buffers)
    return pl.pallas_call(
        functools.partial(stage_body, slot, count, units),
        grid_spec=pltpu.PrefetchScalarGridSpec(
            num_scalar_prefetch=1,
            grid=(count + tiles,),
            in_specs=[anywhere] * 4
            + [
                pl.BlockSpec((stage_rows, units), lambda i, p: (slot, first_part(i))),
                pl.BlockSpec((stage_rows, gates.shape[1]), lambda i, p: (0, 0)),
                pl.BlockSpec((1, width, both_units), lambda i, p: (first_part(i), 0, 0)),
                pl.BlockSpec((count * both_units, tile), lambda i, p: (0, second_part(i))),
            ]
            + [anywhere] * len(previous),
            out_specs=[pl.BlockSpec((rows, tile), lambda i, p: (0, second_part(i)))] * 4
            + [pl.BlockSpec((stage_rows, gates.shape[1]), lambda i, p: (0, 0))]
            + whole_specs,
            scratch_shapes=[
                pltpu.VMEM((stage_rows, width), BRAIN),
                pltpu.VMEM((stage_rows, count * both_units), BRAIN),
                pltpu.SemaphoreType.DMA((4,)),
                pltpu.SemaphoreType.DMA,
            ],
        ),
        out_shape=[jax.ShapeDtypeStruct((rows, width), BRAIN)] * 4
        + [jax.ShapeDtypeStruct((stage_rows, gates.shape[1]), FLOAT)]
        + whole_shapes,
        input_output_aliases={9 + at: 5 + at for at in range(len(previous))},
        compiler_params=pltpu.CompilerParams(dimension_semantics=("arbitrary",)),
        cost_estimate=pl.CostEstimate(
            flops=4 * stage_rows * width * count * both_units,
            bytes_accessed=40 << 20,
            transcendentals=stage_rows * count * units,
        ),
        name="expert_stage",
    )(place, *blocks, down_back, gates, weights, weights_back, *previous)


def back_body(count, *refs):
    blocks = refs[: 4 * count]
    weights, rows_out, back_out, held, in_sems, out_sems = refs[4 * count :]
    step = pl.program_id(0)
    rows = blocks[0].shape[0]

    def incoming(slot):
        return [
            pltpu.make_async_copy(
                blocks[4 * slot + at],
                held.at[slot % 2, pl.ds(at * rows, rows), :],
                in_sems.at[slot % 2, at],
            )
            for at in range(4)
        ]

    def outgoing(slot):
        return pltpu.make_async_copy(
            held.at[slot % 2],
            rows_out.at[pl.ds(slot * 4 * rows, 4 * rows), :],
            out_sems.at[slot % 2],
        )

    for slot in range(count):

        @pl.when(step == slot)
        def _(slot=slot):
            if slot == 0:
                for copy in incoming(0):
                    copy.start()
            if slot > 0:
                outgoing(slot - 1).wait()
            if slot + 1 < count:
                for copy in incoming(slot + 1):
                    copy.start()
            for copy in incoming(slot):
                copy.wait()
            outgoing(slot).start()

    def one(at, carry):
        part = pl.ds(pl.multiple_of(at * rows, rows), rows)
        back_out[part, :] = jnp.dot(
            held[lax.rem(step, 2), part, :], weights[...], preferred_element_type=FLOAT
        ).astype(BRAIN)
        return carry

    lax.fori_loop(0, 4, one, 0)

    @pl.when(step == count - 1)
    def _():
        outgoing(count - 1).wait()


def gathered_back(blocks, weights):
    rows, width = blocks[0].shape
    count = len(blocks) // 4
    units = weights.shape[1]
    anywhere = pl.BlockSpec(memory_space=pl.ANY)
    return pl.pallas_call(
        functools.partial(back_body, count),
        grid=(count,),
        in_specs=[anywhere] * len(blocks) + [pl.BlockSpec((width, units), lambda i: (0, 0))],
        out_specs=[anywhere, pl.BlockSpec((4 * rows, units), lambda i: (i, 0))],
        scratch_shapes=[
            pltpu.VMEM((2, 4 * rows, width), BRAIN),
            pltpu.SemaphoreType.DMA((2, 4)),
            pltpu.SemaphoreType.DMA((2,)),
        ],
        out_shape=[
            jax.ShapeDtypeStruct((4 * rows * count, width), BRAIN),
            jax.ShapeDtypeStruct((4 * rows * count, units), BRAIN),
        ],
        compiler_params=pltpu.CompilerParams(dimension_semantics=("arbitrary",)),
        cost_estimate=pl.CostEstimate(
            flops=8 * rows * count * width * units,
            bytes_accessed=48 << 20,
            transcendentals=0,
        ),
        name="gathered_back",
    )(*blocks, weights)


def placed_body(pairs, units, places, *refs):
    parts, outs = refs[:-2], refs[-2:]
    slots = len(parts) // 2
    for half in (0, 1):
        for slot in range(slots):
            lanes = pl.ds(pl.multiple_of(places[slot] * units, units), units)
            part = parts[half * slots + slot]
            for pair in range(pairs):
                for side in (0, 1):
                    first = (2 * pair + side) * units
                    outs[side][half * pairs + pair, :, lanes] = part[
                        :, first : first + units
                    ].astype(FLOAT)


def placed_grads(places, parts, local_experts, units):
    rows = parts[0].shape[0]
    slots = len(parts) // 2
    shape = (local_experts, rows, slots * units)
    return pl.pallas_call(
        functools.partial(placed_body, local_experts // 2, units),
        in_specs=[pl.BlockSpec(memory_space=pltpu.SMEM)]
        + [pl.BlockSpec(memory_space=pltpu.VMEM)] * len(parts),
        out_specs=[pl.BlockSpec(memory_space=pltpu.VMEM)] * 2,
        out_shape=[jax.ShapeDtypeStruct(shape, FLOAT)] * 2,
        cost_estimate=pl.CostEstimate(
            flops=8 * rows * slots * units, bytes_accessed=12 << 20, transcendentals=0
        ),
        name="placed_grads",
    )(places, *parts)


def swap_over(values, axis, bit):
    count = lax.axis_size(axis)
    return lax.ppermute(values, axis, [(at, at ^ bit) for at in range(count)])


def shift_over(values, axis, steps):
    count = lax.axis_size(axis)
    return lax.ppermute(values, axis, [(at, (at + steps) % count) for at in range(count)])


def axis_bits(axis):
    count = lax.axis_size(axis)
    return [1 << at for at in reversed(range(count.bit_length() - 1))]


def line_shards(
    tokens,
    routes,
    w_query,
    w_key,
    w_value,
    w_out,
    attn_gain,
    query_gain,
    key_gain,
    mlp_gain,
    router,
    w_gate,
    w_up,
    w_down,
    cotangent,
):
    inputs = tokens[0].astype(FLOAT)
    rows, width = inputs.shape
    ctx_count = lax.axis_size(CTX)
    dp_count = lax.axis_size(DP)
    expert_devices = lax.axis_size(EXPERT)
    plane = (DP, EXPERT)
    device_count = ctx_count * dp_count * expert_devices
    local_experts, _, units_all = w_gate.shape
    experts_all = local_experts * expert_devices
    units = units_all // ctx_count
    hidden_units = local_experts * units
    length = rows * ctx_count
    heads = HEADS // ctx_count
    columns = heads * HEAD_DIM
    score_scale = HEAD_DIM ** (-0.5)
    ctx_at = lax.axis_index(CTX)
    dp_at = lax.axis_index(DP)
    expert_at = lax.axis_index(EXPERT)
    first_column = ctx_at * columns
    ring_places = [(ctx_at + ctx_count - slot) % ctx_count for slot in range(ctx_count)]

    attn_inverse = norm_inverse(inputs)
    attn_in = (inputs * attn_inverse * attn_gain).astype(BRAIN)
    all_in = lax.all_gather(attn_in, CTX, axis=0, tiled=True)
    inverses = jnp.concatenate(
        [norm_inverse(times(attn_in, w_query)), norm_inverse(times(attn_in, w_key))], axis=1
    )
    all_inverses = lax.all_gather(inverses, CTX, axis=0, tiled=True)
    query_inverse = all_inverses[:, 0:1]
    key_inverse = all_inverses[:, 1:2]

    qkv_weights = jnp.concatenate(
        [
            lax.dynamic_slice_in_dim(weights, first_column, columns, axis=1)
            for weights in (w_query, w_key, w_value)
        ],
        axis=1,
    )
    query_gain_own = lax.dynamic_slice_in_dim(query_gain, first_column, columns, axis=0)
    key_gain_own = lax.dynamic_slice_in_dim(key_gain, first_column, columns, axis=0)
    cosine, sine_table = rope_tables(jnp.arange(length, dtype=jnp.int32))
    gate_slice, up_slice = [
        lax.dynamic_slice_in_dim(weights, ctx_at * units, units, axis=2)
        for weights in (w_gate, w_up)
    ]
    gate_up_weights = jnp.concatenate([gate_slice, up_slice], axis=2)
    gate_up_back = gate_up_weights.transpose(0, 2, 1).reshape(2 * hidden_units, width)
    down_weights = lax.dynamic_slice_in_dim(w_down, ctx_at * units, units, axis=1).reshape(
        hidden_units, width
    )

    down_across = down_weights.T
    all_in, upstream_low, gate_up_weights, gate_up_back, down_weights, down_across, qkv_weights = (
        meet(
            all_in,
            cotangent[0],
            gate_up_weights,
            gate_up_back,
            down_weights,
            down_across,
            qkv_weights,
        )
    )
    upstream = upstream_low.astype(FLOAT)
    near, far = axis_bits(EXPERT)[::-1]
    up_own = [upstream_low]
    up_own.append(shift_over(up_own[0], CTX, 1))
    up_far = [swap_over(up_own[0], EXPERT, far)]

    qkv_lin = times(all_in, qkv_weights)
    query_lin = qkv_lin[:, :columns]
    key_lin = qkv_lin[:, columns : 2 * columns]
    value_heads = qkv_lin[:, 2 * columns :].astype(BRAIN).reshape(length, heads, HEAD_DIM)
    query_heads = rotated(
        (query_lin * query_inverse * query_gain_own).reshape(length, heads, HEAD_DIM),
        cosine,
        sine_table,
    ).astype(BRAIN)
    key_heads = rotated(
        (key_lin * key_inverse * key_gain_own).reshape(length, heads, HEAD_DIM), cosine, sine_table
    ).astype(BRAIN)
    query_heads, key_heads, up_own[1], up_far[0] = meet(
        query_heads, key_heads, up_own[1], up_far[0]
    )
    up_own.append(shift_over(up_own[1], CTX, 1))
    up_far.append(swap_over(up_own[1], EXPERT, far))
    up_near = [swap_over(up_own[0], EXPERT, near)]
    up_both = [swap_over(up_far[0], EXPERT, near)]
    positions = jnp.arange(length, dtype=jnp.int32)
    visible = (positions[None, :] <= positions[:, None])[None]
    scores = (
        jnp.einsum("qhd,khd->hqk", query_heads, key_heads, preferred_element_type=FLOAT)
        * score_scale
    )
    scores = jnp.where(visible, scores, -1e30)
    probs = jax.nn.softmax(scores, axis=-1)
    probs_low = probs.astype(BRAIN)
    attn_wide = jnp.einsum("hqk,khd->qhd", probs_low, value_heads, preferred_element_type=FLOAT)
    attn_own = attn_wide.astype(BRAIN).reshape(length, columns)
    attn_own, up_own, up_far, up_near, up_both = meet(attn_own, up_own, up_far, up_near, up_both)
    up_far.append(swap_over(up_own[2], EXPERT, far))
    up_near.append(swap_over(up_own[1], EXPERT, near))
    up_near.append(swap_over(up_own[2], EXPERT, near))
    up_both.append(swap_over(up_far[1], EXPERT, near))
    attn_rows = lax.all_to_all(attn_own, CTX, split_axis=0, concat_axis=1, tiled=True)
    attn_rows, up_own, up_far, up_near, up_both = meet(
        attn_rows, up_own, up_far, up_near, up_both
    )
    up_own.append(shift_over(up_own[2], CTX, 1))
    up_both.append(swap_over(up_far[2], EXPERT, near))
    up_far.append(swap_over(up_own[3], EXPERT, far))
    up_near.append(swap_over(up_own[3], EXPERT, near))
    hidden = inputs + times(attn_rows, w_out)
    mlp_inverse = norm_inverse(hidden)
    expert_in = (hidden * mlp_inverse * mlp_gain).astype(BRAIN)
    logits = times(expert_in, router)
    gate_probs = jax.nn.softmax(logits, axis=-1)
    chosen = jnp.any(
        routes[0][:, :, None] == jnp.arange(experts_all, dtype=jnp.int32)[None, None, :], axis=1
    )
    gates = jnp.where(chosen, gate_probs, 0.0).astype(BRAIN)

    def dp_parts(partial, outer, inner):
        halves = partial.reshape(outer, dp_count, inner, -1)
        return (
            lax.dynamic_index_in_dim(halves, dp_at, axis=1, keepdims=False),
            swap_over(
                lax.dynamic_index_in_dim(halves, 1 - dp_at, axis=1, keepdims=False), DP, 1
            ),
        )

    def ctx_parts(blocks):
        return [
            shift_over(
                lax.dynamic_index_in_dim(
                    blocks, (ctx_at + at) % ctx_count, axis=0, keepdims=False
                ),
                CTX,
                at,
            )
            if at
            else lax.dynamic_index_in_dim(blocks, ctx_at, axis=0, keepdims=False)
            for at in range(ctx_count)
        ]

    grad_rows = width // (ctx_count * dp_count)
    padded_gates = jnp.pad(gates, ((0, 0), (0, -experts_all % 128)))
    first_expert = expert_at * local_experts
    expert_place = jnp.full((1,), first_expert, jnp.int32)

    moved_own = [expert_in]
    moved_far, moved_near, moved_both = [], [], []
    gate_slots, stages, near_sums, far_sums, half_grads = [], [], [], [], []
    buffers = produced = sent = total = total_gate = None
    gate_half = padded_gates
    for tick in range(ctx_count + 5):
        slot = tick - 2
        fresh = {}
        if tick + 1 < ctx_count:
            fresh[OWN] = shift_over(moved_own[tick], CTX, 1)
        if tick < ctx_count:
            fresh[FAR] = swap_over(moved_own[tick], EXPERT, far)
            fresh[NEAR] = swap_over(moved_own[tick], EXPERT, near)
        if 0 <= tick - 1 < ctx_count:
            fresh[BOTH] = swap_over(moved_far[tick - 1], EXPERT, near)
        if tick == 0:
            fresh[GATES] = jnp.concatenate([gate_half, swap_over(gate_half, EXPERT, far)])
            fresh[UP_BOTH] = swap_over(up_far[3], EXPERT, near)
        if tick == 1:
            fresh[GATES] = jnp.concatenate([gate_half, swap_over(gate_half, EXPERT, near)])
            fresh[BACK] = gathered_back(
                [
                    kind[at]
                    for at in range(ctx_count)
                    for kind in (up_own, up_far, up_near, up_both)
                ],
                down_across,
            )
        if 2 <= tick < ctx_count + 1:
            fresh[GATES] = shift_over(gate_slots[-1], CTX, 1)
        if 0 <= slot < ctx_count:
            fresh[STAGE] = expert_stage(
                slot,
                expert_place,
                (moved_own[slot], moved_far[slot], moved_near[slot], moved_both[slot]),
                down_back,
                gate_slots[slot],
                gate_up_weights,
                gate_up_back,
                buffers,
            )
        if 0 <= slot - 1 < ctx_count:
            grads = stages[slot - 1]
            gate_part = grads[4].astype(BRAIN)
            fresh[NEAR_SUM] = (
                grads[0] + swap_over(grads[2], EXPERT, near),
                grads[1] + swap_over(grads[3], EXPERT, near),
                gate_part[: 2 * rows] + swap_over(gate_part[2 * rows :], EXPERT, near),
            )
        if 0 <= slot - 2 < ctx_count:
            pair = near_sums[slot - 2]
            fresh[FAR_SUM] = (
                pair[0] + swap_over(pair[1], EXPERT, far),
                pair[2][:rows] + swap_over(pair[2][rows:], EXPERT, far),
            )
        if tick == ctx_count + 2:
            total, total_gate = far_sums[1]
            all_rows, all_pre_grads, all_weighted = buffers
            fresh[MADE] = [
                [
                    times(
                        all_weighted[(4 * at + 2 * part) * rows :][: 2 * rows], down_weights
                    ).astype(BRAIN)
                    for part in (0, 1)
                ]
                for at in range(ctx_count)
            ]
        if tick >= ctx_count + 2:
            fresh[RING] = (shift_over(total, CTX, 1), shift_over(total_gate, CTX, 1))
        if tick == ctx_count + 3:
            fresh[MADE] = []
            for kept, given in produced:
                taken = swap_over(given, EXPERT, near)
                fresh[MADE].append((kept[:rows] + taken[:rows], kept[rows:] + taken[rows:]))
        if tick == ctx_count + 4:
            fresh[MADE] = [produced[1][0] + swap_over(produced[1][1], EXPERT, far), produced]
            first_parts = dp_parts(half_grads[0], ctx_count, grad_rows)
        if tick >= ctx_count + 3:
            half = tick - ctx_count - 3
            fresh[HALF] = outer_sum(
                all_rows, all_pre_grads[:, half * hidden_units :][:, :hidden_units]
            ).astype(BRAIN)
        fresh = meet(fresh)[0]
        if OWN in fresh:
            moved_own.append(fresh[OWN])
        if FAR in fresh:
            moved_far.append(fresh[FAR])
            moved_near.append(fresh[NEAR])
        if BOTH in fresh:
            moved_both.append(fresh[BOTH])
        if tick == 0:
            up_both.append(fresh[UP_BOTH])
            gate_half = fresh[GATES]
        elif GATES in fresh:
            gate_slots.append(fresh[GATES])
        if BACK in fresh:
            all_upstream, down_back = fresh[BACK]
        if STAGE in fresh:
            stages.append(fresh[STAGE][:5])
            buffers = fresh[STAGE][5:]
        if NEAR_SUM in fresh:
            near_sums.append(fresh[NEAR_SUM])
        if FAR_SUM in fresh:
            far_sums.append(fresh[FAR_SUM])
        if RING in fresh:
            following = far_sums[(tick - ctx_count) % ctx_count]
            total = fresh[RING][0] + following[0]
            total_gate = fresh[RING][1] + following[1]
        if MADE in fresh:
            produced = fresh[MADE]
        if HALF in fresh:
            half_grads.append(fresh[HALF])
    expert_in_grad = total.astype(FLOAT)
    gate_grads = total_gate[:, :experts_all].astype(FLOAT)
    produced_total, produced = produced

    prob_grads = jnp.where(chosen, gate_grads, 0.0)
    logit_grads = (
        gate_probs * (prob_grads - jnp.sum(prob_grads * gate_probs, axis=-1, keepdims=True))
    ).astype(BRAIN)
    router_grad = outer_sum(expert_in, logit_grads)
    expert_in_grad = expert_in_grad + times_transpose(logit_grads, router)
    hidden_part, mlp_gain_grad = norm_backward(hidden, mlp_inverse, mlp_gain, expert_in_grad)
    hidden_grad = upstream + hidden_part
    hidden_low = hidden_grad.astype(BRAIN)
    attn_grad_rows = times_transpose(hidden_low, w_out).astype(BRAIN)
    second_parts = dp_parts(half_grads[1], ctx_count, grad_rows)
    produced_two = produced[2][0] + swap_over(produced[2][1], EXPERT, far)
    produced_three = produced[3][0] + swap_over(produced[3][1], EXPERT, far)
    produced_total = shift_over(produced_total, CTX, 1)
    attn_grad_rows, first_parts = meet(attn_grad_rows, first_parts)
    attn_grad = lax.all_to_all(
        attn_grad_rows.reshape(rows, ctx_count, columns).transpose(1, 0, 2),
        CTX,
        split_axis=0,
        concat_axis=0,
        tiled=True,
    ).reshape(length, columns)
    first_half = ctx_parts(first_parts[0] + first_parts[1])
    down_half = outer_sum(all_weighted, all_upstream).astype(BRAIN)
    attn_grad, produced_two, produced_three, down_half, produced, hidden_low, produced_total = meet(
        attn_grad, produced_two, produced_three, down_half, produced, hidden_low, produced_total
    )
    attn_grad_heads = attn_grad.reshape(length, heads, HEAD_DIM)
    out_weight_grad = outer_sum(attn_rows, hidden_low).astype(BRAIN)
    out_weight_grad = lax.psum_scatter(
        out_weight_grad.reshape(ctx_count, width // ctx_count, width),
        plane,
        scatter_dimension=1,
        tiled=True,
    )
    produced_zero = produced[0][0] + swap_over(produced[0][1], EXPERT, far)
    produced_total = shift_over(produced_total + produced_two, CTX, 1)
    row_delta = jnp.sum(attn_wide * attn_grad_heads.astype(FLOAT), axis=-1).T
    prob_grad = jnp.einsum(
        "qhd,khd->hqk", attn_grad_heads, value_heads, preferred_element_type=FLOAT
    )
    score_grad = (probs * (prob_grad - row_delta[..., None])).astype(BRAIN)
    score_grad, produced_total, second_parts = meet(score_grad, produced_total, second_parts)
    produced_total = shift_over(produced_total + produced_three, CTX, 1)
    second_half = ctx_parts(second_parts[0] + second_parts[1])
    down_parts = dp_parts(down_half, local_experts, units // dp_count)
    query_grad = (
        jnp.einsum("hqk,khd->qhd", score_grad, key_heads, preferred_element_type=FLOAT)
        * score_scale
    )
    key_grad = (
        jnp.einsum("hqk,qhd->khd", score_grad, query_heads, preferred_element_type=FLOAT)
        * score_scale
    )
    value_low = (
        jnp.einsum("hqk,qhd->khd", probs_low, attn_grad_heads, preferred_element_type=FLOAT)
        .astype(BRAIN)
        .reshape(length, columns)
    )
    query_grad, key_grad, value_low = meet(query_grad, key_grad, value_low)
    query_rot_grad = rotated_back(query_grad, cosine, sine_table).reshape(length, columns)
    key_rot_grad = rotated_back(key_grad, cosine, sine_table).reshape(length, columns)
    query_weighted = query_rot_grad * query_gain_own
    key_weighted = key_rot_grad * key_gain_own
    dots = jnp.stack(
        [jnp.sum(query_weighted * query_lin, axis=-1), jnp.sum(key_weighted * key_lin, axis=-1)]
    )
    dots = lax.psum(dots, CTX) * (1.0 / width)
    query_gain_grad = jnp.sum(query_rot_grad * query_lin * query_inverse, axis=0)
    key_gain_grad = jnp.sum(key_rot_grad * key_lin * key_inverse, axis=0)
    query_low = (
        query_inverse * query_weighted
        - query_lin * (query_inverse * query_inverse * query_inverse * dots[0][:, None])
    ).astype(BRAIN)
    key_low = (
        key_inverse * key_weighted
        - key_lin * (key_inverse * key_inverse * key_inverse * dots[1][:, None])
    ).astype(BRAIN)
    qkv_low = jnp.concatenate([query_low, key_low, value_low], axis=1)
    qkv_low, produced_total, out_weight_grad, first_half, second_half, down_parts, produced_zero = (
        meet(
            qkv_low,
            produced_total,
            out_weight_grad,
            first_half,
            second_half,
            down_parts,
            produced_zero,
        )
    )
    produced_total = produced_total + produced_zero
    mixed = hidden + produced_total.astype(FLOAT)
    down_weight_grad = (down_parts[0] + down_parts[1]).astype(FLOAT)
    out_weight_grad = sum(
        (
            part.astype(FLOAT)
            for part in ctx_parts(out_weight_grad)
        ),
        jnp.zeros(out_weight_grad.shape[1:], FLOAT),
    )

    attn_in_parts = times_transpose(qkv_low, qkv_weights)
    attn_gain_grad = jnp.sum(attn_in_parts * all_in.astype(FLOAT), axis=0) / attn_gain
    attn_in_low = attn_in_parts.astype(BRAIN)
    attn_in_slots = [
        lax.dynamic_slice_in_dim(attn_in_low, place * rows, rows, axis=0) for place in ring_places
    ]
    attn_in_total = shift_over(attn_in_slots[1], CTX, 1)
    attn_in_total = attn_in_total + attn_in_slots[2]
    attn_in_total = shift_over(attn_in_total, CTX, 1) + attn_in_slots[3]
    attn_in_grad = (shift_over(attn_in_total, CTX, 1) + attn_in_slots[0]).astype(FLOAT)
    gate_weight_grad, up_weight_grad = placed_grads(
        jnp.stack(ring_places).astype(jnp.int32), first_half + second_half, local_experts, units
    )

    empty = jnp.zeros((width,), FLOAT)
    small = jnp.concatenate(
        [
            jnp.stack(
                [
                    attn_gain_grad,
                    lax.dynamic_update_slice_in_dim(empty, query_gain_grad, first_column, axis=0),
                    lax.dynamic_update_slice_in_dim(empty, key_gain_grad, first_column, axis=0),
                    mlp_gain_grad,
                ],
                axis=0,
            ),
            router_grad.T,
        ],
        axis=0,
    )
    own_width = width // device_count
    small_count = 4 + experts_all
    small = small.reshape(small_count, device_count, own_width).transpose(1, 0, 2)
    small = small.reshape(ctx_count, dp_count, 2, 2, small_count * own_width // 128, 128)
    for axis, bit, mine, place in (
        (DP, 1, dp_at, 1),
        (EXPERT, far, expert_at // 2, 1),
        (EXPERT, near, expert_at % 2, 1),
    ):
        kept = lax.dynamic_index_in_dim(small, mine, axis=place, keepdims=False)
        given = lax.dynamic_index_in_dim(small, 1 - mine, axis=place, keepdims=False)
        small = kept + swap_over(given, axis, bit)
    small = sum(ctx_parts(small)).reshape(small_count, own_width)
    qkv_weight_grad = outer_sum(all_in, qkv_low).astype(BRAIN)
    qkv_weight_grad = lax.psum_scatter(
        qkv_weight_grad.reshape(ctx_count, width // ctx_count, 3 * columns),
        plane,
        scatter_dimension=1,
        tiled=True,
    )
    qkv_weight_grad = lax.all_to_all(qkv_weight_grad, CTX, split_axis=0, concat_axis=0, tiled=True)
    qkv_weight_grad = (
        qkv_weight_grad.reshape(ctx_count, own_width, 3, columns)
        .transpose(2, 1, 0, 3)
        .reshape(3, own_width, width)
        .astype(FLOAT)
    )
    input_part, _ = norm_backward(inputs, attn_inverse, attn_gain, attn_in_grad)
    input_grad = hidden_grad + input_part

    return (
        mixed.astype(BRAIN)[None],
        input_grad[None],
        qkv_weight_grad[0],
        qkv_weight_grad[1],
        qkv_weight_grad[2],
        out_weight_grad,
        small[0],
        small[1],
        small[2],
        small[3],
        small[4:].T,
        gate_weight_grad,
        up_weight_grad,
        down_weight_grad,
    )


def solution(mesh):
    sizes = mesh.shape
    if not (sizes[CTX] == 4 and sizes[EXPERT] == 4 and sizes[DP] == 2):
        return placed_over(mesh, plane_shards)

    return placed_over(mesh, line_shards)


def placed_over(mesh, shards):
    return jax.shard_map(
        shards,
        mesh=mesh,
        in_specs=(
            P((DP, EXPERT), CTX, None),
            P((DP, EXPERT), CTX, None),
            P(),
            P(),
            P(),
            P(),
            P(),
            P(),
            P(),
            P(),
            P(),
            P(EXPERT, None, None),
            P(EXPERT, None, None),
            P(EXPERT, None, None),
            P((DP, EXPERT), CTX, None),
        ),
        out_specs=(
            P((DP, EXPERT), CTX, None),
            P((DP, EXPERT), CTX, None),
            P((CTX, DP, EXPERT), None),
            P((CTX, DP, EXPERT), None),
            P((CTX, DP, EXPERT), None),
            P((CTX, DP, EXPERT), None),
            P((CTX, DP, EXPERT)),
            P((CTX, DP, EXPERT)),
            P((CTX, DP, EXPERT)),
            P((CTX, DP, EXPERT)),
            P((CTX, DP, EXPERT), None),
            P(EXPERT, (CTX, DP), None),
            P(EXPERT, (CTX, DP), None),
            P(EXPERT, (CTX, DP), None),
        ),
        check_vma=False,
    )
```

```python
import functools

import jax
import jax.numpy as jnp
from jax import lax
from jax.experimental import pallas as pl
from jax.experimental.pallas import tpu as pltpu
from jax.sharding import PartitionSpec as P


HEADS = 16
HEAD_DIM = 128


EPSILON = 1e-05
FLOAT = jnp.float32
BRAIN = jnp.bfloat16
CTX = "ctx"
DP = "dp"
EXPERT = "expert"
OWN, FAR, NEAR, BOTH, GATES, UP_BOTH, BACK, STAGE = range(8)
NEAR_SUM, FAR_SUM, MADE, RING, HALF, DGATE = range(8, 14)


def norm_inverse(values):
    return lax.rsqrt(jnp.mean(values * values, axis=-1, keepdims=True) + EPSILON)


def norm_backward(values, inverse, gain, upstream):
    weighted = upstream * gain
    gain_grad = jnp.sum(upstream * values * inverse, axis=0)
    value_grad = inverse * weighted - values * inverse * inverse * inverse * jnp.mean(
        weighted * values, axis=-1, keepdims=True
    )
    return (value_grad, gain_grad)


def rope_tables(positions):
    halfway = HEAD_DIM // 2
    frequency = 10000.0 ** (-jnp.arange(halfway, dtype=FLOAT) * 2.0 / HEAD_DIM)
    angles = positions.astype(FLOAT)[:, None] * frequency[None, :]
    angles = jnp.concatenate([angles, angles], axis=1)
    return (jnp.cos(angles), jnp.sin(angles))


def rotated(heads_rows, cosine, sine_table):
    halfway = HEAD_DIM // 2
    turned = jnp.concatenate([-heads_rows[..., halfway:], heads_rows[..., :halfway]], axis=-1)
    return heads_rows * cosine[:, None, :] + turned * sine_table[:, None, :]


def rotated_back(grads, cosine, sine_table):
    halfway = HEAD_DIM // 2
    sined = grads * sine_table[:, None, :]
    return grads * cosine[:, None, :] + jnp.concatenate(
        [sined[..., halfway:], -sined[..., :halfway]], axis=-1
    )


def outer_sum(left, right):
    return lax.dot_general(left, right, (((0,), (0,)), ((), ())), preferred_element_type=FLOAT)


def times_transpose(left, right):
    return lax.dot_general(left, right, (((1,), (1,)), ((), ())), preferred_element_type=FLOAT)


def times(left, right):
    return jnp.dot(left, right, preferred_element_type=FLOAT)


def plane_shards(
    tokens,
    routes,
    w_query,
    w_key,
    w_value,
    w_out,
    attn_gain,
    query_gain,
    key_gain,
    mlp_gain,
    router,
    w_gate,
    w_up,
    w_down,
    cotangent,
):
    inputs = tokens[0].astype(FLOAT)
    rows, width = inputs.shape
    ctx_count = lax.axis_size(CTX)
    dp_count = lax.axis_size(DP)
    expert_devices = lax.axis_size(EXPERT)
    plane = (DP, EXPERT)
    plane_count = dp_count * expert_devices
    everything = (CTX, DP, EXPERT)
    local_experts = w_gate.shape[0]
    experts_all = local_experts * expert_devices
    own_experts = local_experts // dp_count
    length = rows * ctx_count
    heads = HEADS // ctx_count
    columns = heads * HEAD_DIM
    score_scale = HEAD_DIM ** (-0.5)
    ctx_at = lax.axis_index(CTX)
    dp_at = lax.axis_index(DP)
    expert_at = lax.axis_index(EXPERT)
    first_column = ctx_at * columns

    attn_inverse = norm_inverse(inputs)
    attn_in = (inputs * attn_inverse * attn_gain).astype(BRAIN)
    all_in = lax.all_gather(attn_in, CTX, axis=0, tiled=True)
    upstream_low = cotangent[0]
    upstream = upstream_low.astype(FLOAT)
    all_upstream = lax.all_gather(upstream_low, plane, axis=0, tiled=True)

    qkv_weights = jnp.concatenate(
        [
            lax.dynamic_slice_in_dim(weights, first_column, columns, axis=1)
            for weights in (w_query, w_key, w_value)
        ],
        axis=1,
    )
    out_weights = lax.dynamic_slice_in_dim(w_out, first_column, columns, axis=0)
    query_gain_own = lax.dynamic_slice_in_dim(query_gain, first_column, columns, axis=0)
    key_gain_own = lax.dynamic_slice_in_dim(key_gain, first_column, columns, axis=0)
    inverses = jnp.concatenate(
        [norm_inverse(times(attn_in, w_query)), norm_inverse(times(attn_in, w_key))], axis=1
    )
    all_inverses = lax.all_gather(inverses, CTX, axis=0, tiled=True)
    query_inverse = all_inverses[:, 0:1]
    key_inverse = all_inverses[:, 1:2]
    cosine, sine_table = rope_tables(jnp.arange(length, dtype=jnp.int32))

    gate_weights, up_weights, down_weights = [
        lax.dynamic_slice_in_dim(weights, dp_at * own_experts, own_experts, axis=0)
        for weights in (w_gate, w_up, w_down)
    ]
    down_back = jnp.einsum(
        "td,efd->etf", all_upstream, down_weights, preferred_element_type=FLOAT
    )

    qkv_lin = times(all_in, qkv_weights)
    query_lin = qkv_lin[:, :columns]
    key_lin = qkv_lin[:, columns : 2 * columns]
    value_heads = qkv_lin[:, 2 * columns :].astype(BRAIN).reshape(length, heads, HEAD_DIM)
    query_heads = rotated(
        (query_lin * query_inverse * query_gain_own).reshape(length, heads, HEAD_DIM),
        cosine,
        sine_table,
    ).astype(BRAIN)
    key_heads = rotated(
        (key_lin * key_inverse * key_gain_own).reshape(length, heads, HEAD_DIM), cosine, sine_table
    ).astype(BRAIN)
    positions = jnp.arange(length, dtype=jnp.int32)
    visible = (positions[None, :] <= positions[:, None])[None]
    scores = (
        jnp.einsum("qhd,khd->hqk", query_heads, key_heads, preferred_element_type=FLOAT)
        * score_scale
    )
    scores = jnp.where(visible, scores, -1e30)
    probs = jax.nn.softmax(scores, axis=-1)
    probs_low = probs.astype(BRAIN)
    attn_wide = jnp.einsum("hqk,khd->qhd", probs_low, value_heads, preferred_element_type=FLOAT)
    attn_own = attn_wide.astype(BRAIN).reshape(length, columns)
    attn_rows = lax.all_to_all(attn_own, CTX, split_axis=0, concat_axis=1, tiled=True)
    hidden = inputs + times(attn_rows, w_out)
    mlp_inverse = norm_inverse(hidden)
    expert_in = (hidden * mlp_inverse * mlp_gain).astype(BRAIN)
    all_expert_in = lax.all_gather(expert_in, plane, axis=0, tiled=True)
    logits = times(expert_in, router)
    gate_probs = jax.nn.softmax(logits, axis=-1)
    chosen = jnp.any(
        routes[0][:, :, None] == jnp.arange(experts_all, dtype=jnp.int32)[None, None, :], axis=1
    )
    gates = jnp.where(chosen, gate_probs, 0.0)
    all_gates = lax.all_gather(gates, plane, axis=0, tiled=True)
    first_expert = expert_at * local_experts + dp_at * own_experts
    own_gates = lax.dynamic_slice_in_dim(all_gates, first_expert, own_experts, axis=1).T[:, :, None]

    gate_pre = jnp.einsum(
        "td,edf->etf", all_expert_in, gate_weights, preferred_element_type=FLOAT
    )
    up_pre = jnp.einsum("td,edf->etf", all_expert_in, up_weights, preferred_element_type=FLOAT)
    sigmoid_gate = jax.nn.sigmoid(gate_pre)
    silu_gate = gate_pre * sigmoid_gate
    activated = silu_gate * up_pre
    weighted = (own_gates * activated).astype(BRAIN)
    own_gate_grads = jnp.sum(down_back * activated, axis=-1).T
    act_grad = own_gates * down_back
    up_grad = (act_grad * silu_gate).astype(BRAIN)
    gate_grad = (act_grad * up_pre * sigmoid_gate * (1.0 + gate_pre * (1.0 - sigmoid_gate))).astype(
        BRAIN
    )
    input_rows = (
        jnp.einsum("etf,edf->td", gate_grad, gate_weights, preferred_element_type=FLOAT)
        + jnp.einsum("etf,edf->td", up_grad, up_weights, preferred_element_type=FLOAT)
    ).astype(BRAIN)
    expert_in_grad = lax.psum_scatter(input_rows, plane, scatter_dimension=0, tiled=True).astype(
        FLOAT
    )
    produced = jnp.einsum(
        "etf,efd->td", weighted, down_weights, preferred_element_type=FLOAT
    ).astype(BRAIN)
    mixed = hidden + lax.psum_scatter(produced, plane, scatter_dimension=0, tiled=True).astype(
        FLOAT
    )
    gate_grads = lax.all_to_all(
        own_gate_grads.reshape(plane_count, rows, own_experts),
        plane,
        split_axis=0,
        concat_axis=0,
        tiled=True,
    )
    gate_grads = (
        gate_grads.reshape(dp_count, expert_devices, rows, own_experts)
        .transpose(2, 1, 0, 3)
        .reshape(rows, experts_all)
    )

    def spread(partial):
        summed = lax.psum_scatter(partial.astype(BRAIN), CTX, scatter_dimension=1, tiled=True)
        return lax.all_to_all(summed, DP, split_axis=1, concat_axis=0, tiled=True).astype(FLOAT)

    down_weight_grad = spread(
        jnp.einsum("etf,td->efd", weighted, all_upstream, preferred_element_type=FLOAT)
    )
    gate_weight_grad = spread(
        jnp.einsum("td,etf->edf", all_expert_in, gate_grad, preferred_element_type=FLOAT)
    )
    up_weight_grad = spread(
        jnp.einsum("td,etf->edf", all_expert_in, up_grad, preferred_element_type=FLOAT)
    )

    prob_grads = jnp.where(chosen, gate_grads, 0.0)
    logit_grads = (
        gate_probs * (prob_grads - jnp.sum(prob_grads * gate_probs, axis=-1, keepdims=True))
    ).astype(BRAIN)
    router_grad = outer_sum(expert_in, logit_grads)
    expert_in_grad = expert_in_grad + times_transpose(logit_grads, router)
    hidden_part, mlp_gain_grad = norm_backward(hidden, mlp_inverse, mlp_gain, expert_in_grad)
    hidden_grad = upstream + hidden_part
    hidden_low = hidden_grad.astype(BRAIN)
    all_hidden_low = lax.all_gather(hidden_low, CTX, axis=0, tiled=True)
    attn_grad = times_transpose(all_hidden_low, out_weights).astype(BRAIN)
    attn_grad_heads = attn_grad.reshape(length, heads, HEAD_DIM)
    out_weight_grad = lax.psum_scatter(
        outer_sum(attn_own, all_hidden_low).astype(BRAIN), plane, scatter_dimension=0, tiled=True
    ).astype(FLOAT)
    row_delta = jnp.sum(attn_wide * attn_grad_heads.astype(FLOAT), axis=-1).T
    prob_grad = jnp.einsum(
        "qhd,khd->hqk", attn_grad_heads, value_heads, preferred_element_type=FLOAT
    )
    score_grad = (probs * (prob_grad - row_delta[..., None])).astype(BRAIN)
    query_grad = (
        jnp.einsum("hqk,khd->qhd", score_grad, key_heads, preferred_element_type=FLOAT)
        * score_scale
    )
    key_grad = (
        jnp.einsum("hqk,qhd->khd", score_grad, query_heads, preferred_element_type=FLOAT)
        * score_scale
    )
    value_low = (
        jnp.einsum("hqk,qhd->khd", probs_low, attn_grad_heads, preferred_element_type=FLOAT)
        .astype(BRAIN)
        .reshape(length, columns)
    )
    query_rot_grad = rotated_back(query_grad, cosine, sine_table).reshape(length, columns)
    key_rot_grad = rotated_back(key_grad, cosine, sine_table).reshape(length, columns)
    query_weighted = query_rot_grad * query_gain_own
    key_weighted = key_rot_grad * key_gain_own
    dots = lax.psum(
        jnp.stack(
            [jnp.sum(query_weighted * query_lin, axis=-1), jnp.sum(key_weighted * key_lin, axis=-1)]
        ),
        CTX,
    ) * (1.0 / width)
    query_gain_grad = jnp.sum(query_rot_grad * query_lin * query_inverse, axis=0)
    key_gain_grad = jnp.sum(key_rot_grad * key_lin * key_inverse, axis=0)
    query_low = (
        query_inverse * query_weighted
        - query_lin * (query_inverse * query_inverse * query_inverse * dots[0][:, None])
    ).astype(BRAIN)
    key_low = (
        key_inverse * key_weighted
        - key_lin * (key_inverse * key_inverse * key_inverse * dots[1][:, None])
    ).astype(BRAIN)
    qkv_low = jnp.concatenate([query_low, key_low, value_low], axis=1)
    attn_in_grad = lax.psum_scatter(
        times_transpose(qkv_low, qkv_weights).astype(BRAIN), CTX, scatter_dimension=0, tiled=True
    ).astype(FLOAT)
    qkv_weight_grad = outer_sum(all_in, qkv_low).astype(BRAIN)
    qkv_weight_grad = lax.psum_scatter(
        qkv_weight_grad.reshape(ctx_count, width // ctx_count, 3 * columns),
        plane,
        scatter_dimension=1,
        tiled=True,
    )
    qkv_weight_grad = lax.all_to_all(
        qkv_weight_grad, CTX, split_axis=0, concat_axis=0, tiled=True
    )
    out_rows = qkv_weight_grad.shape[1]
    qkv_weight_grad = (
        qkv_weight_grad.reshape(ctx_count, out_rows, 3, columns)
        .transpose(2, 1, 0, 3)
        .reshape(3, out_rows, width)
        .astype(FLOAT)
    )
    input_part, attn_gain_grad = norm_backward(inputs, attn_inverse, attn_gain, attn_in_grad)
    input_grad = hidden_grad + input_part

    empty = jnp.zeros((width,), FLOAT)
    small = jnp.concatenate(
        [
            jnp.stack(
                [
                    attn_gain_grad,
                    lax.dynamic_update_slice_in_dim(empty, query_gain_grad, first_column, axis=0),
                    lax.dynamic_update_slice_in_dim(empty, key_gain_grad, first_column, axis=0),
                    mlp_gain_grad,
                ],
                axis=1,
            ),
            router_grad,
        ],
        axis=1,
    )
    small = lax.psum_scatter(small, everything, scatter_dimension=0, tiled=True)
    return (
        mixed.astype(BRAIN)[None],
        input_grad[None],
        qkv_weight_grad[0],
        qkv_weight_grad[1],
        qkv_weight_grad[2],
        out_weight_grad,
        small[:, 0],
        small[:, 1],
        small[:, 2],
        small[:, 3],
        small[:, 4:],
        gate_weight_grad,
        up_weight_grad,
        down_weight_grad,
    )


def meet(*values):
    return lax.optimization_barrier(values)


def stage_body(
    slot,
    count,
    units,
    place,
    own,
    far,
    near,
    both,
    back,
    gates,
    weights,
    weights_back,
    *rest,
):
    row_outs = rest[-12:-8]
    gate_grads_out, rows_out, grads_out, weighted_out = rest[-8:-4]
    held, grads, in_sems, out_sem = rest[-4:]
    step = pl.program_id(0)
    rows = own.shape[0]
    whole = rows_out.at[pl.ds(slot * 4 * rows, 4 * rows), :]

    @pl.when(step == 0)
    def _():
        copies = [
            pltpu.make_async_copy(block, held.at[pl.ds(at * rows, rows), :], in_sems.at[at])
            for at, block in enumerate((own, far, near, both))
        ]
        for copy in copies:
            copy.start()
        gate_grads_out[...] = jnp.zeros_like(gate_grads_out)
        for copy in copies:
            copy.wait()
        pltpu.make_async_copy(held, whole, out_sem).start()

    @pl.when(step < count)
    def _():
        lane = lax.broadcasted_iota(jnp.int32, (rows, gates.shape[1]), 1)
        wanted = lane == place[0] + step

        def one(at, carry):
            part = pl.ds(pl.multiple_of(at * rows, rows), rows)
            pre = jnp.dot(held[part, :], weights[0], preferred_element_type=FLOAT)
            gate_pre, up_pre = pre[:, :units], pre[:, units:]
            down_back = back[part, :].astype(FLOAT)
            gate = jnp.sum(
                jnp.where(wanted, gates[part, :].astype(FLOAT), 0.0), axis=1, keepdims=True
            )
            sigmoid = jax.nn.sigmoid(gate_pre)
            silu = gate_pre * sigmoid
            activated = silu * up_pre
            inner = pl.ds(pl.multiple_of(lax.rem(at, 2) * rows, rows), rows)
            weighted_out[lax.div(at, 2), inner, :] = (gate * activated).astype(BRAIN)
            gate_grad = jnp.sum(down_back * activated, axis=1, keepdims=True)
            gate_grads_out[part, :] += jnp.where(wanted, gate_grad, 0.0)
            act_grad = gate * down_back
            gate_side = (
                act_grad * up_pre * sigmoid * (1.0 + gate_pre * (1.0 - sigmoid))
            ).astype(BRAIN)
            up_side = (act_grad * silu).astype(BRAIN)
            grads_out[part, :units] = gate_side
            grads_out[part, units:] = up_side
            first = pl.multiple_of(step * 2 * units, 2 * units)
            grads[part, pl.ds(first, units)] = gate_side
            grads[part, pl.ds(first + units, units)] = up_side
            return carry

        lax.fori_loop(0, 4, one, 0, unroll=4)

    @pl.when(step >= count)
    def _():
        for at in range(4):
            row_outs[at][...] = jnp.dot(
                grads[at * rows : (at + 1) * rows, :],
                weights_back[...],
                preferred_element_type=FLOAT,
            ).astype(BRAIN)

    @pl.when(step == pl.num_programs(0) - 1)
    def _():
        pltpu.make_async_copy(held, whole, out_sem).wait()


def expert_stage(slot, place, blocks, down_back, gates, weights, weights_back, buffers):
    rows, width = blocks[0].shape
    count, _, both_units = weights.shape
    units = both_units // 2
    stage_rows = 4 * rows
    tiles = 4
    tile = width // tiles
    all_rows = down_back.shape[0]
    anywhere = pl.BlockSpec(memory_space=pl.ANY)

    def first_part(step):
        return jnp.minimum(step, count - 1)

    def second_part(step):
        return jnp.maximum(step - count, 0)

    whole_specs = [
        anywhere,
        pl.BlockSpec((stage_rows, both_units), lambda i, p: (slot, first_part(i))),
        pl.BlockSpec((2, stage_rows // 2, units), lambda i, p: (0, slot, first_part(i))),
    ]
    whole_shapes = [
        jax.ShapeDtypeStruct((all_rows, width), BRAIN),
        jax.ShapeDtypeStruct((all_rows, count * both_units), BRAIN),
        jax.ShapeDtypeStruct((2, all_rows // 2, count * units), BRAIN),
    ]
    previous = () if buffers is None else tuple(buffers)
    return pl.pallas_call(
        functools.partial(stage_body, slot, count, units),
        grid_spec=pltpu.PrefetchScalarGridSpec(
            num_scalar_prefetch=1,
            grid=(count + tiles,),
            in_specs=[anywhere] * 4
            + [
                pl.BlockSpec((stage_rows, units), lambda i, p: (slot, first_part(i))),
                pl.BlockSpec((stage_rows, gates.shape[1]), lambda i, p: (0, 0)),
                pl.BlockSpec((1, width, both_units), lambda i, p: (first_part(i), 0, 0)),
                pl.BlockSpec((count * both_units, tile), lambda i, p: (0, second_part(i))),
            ]
            + [anywhere] * len(previous),
            out_specs=[pl.BlockSpec((rows, tile), lambda i, p: (0, second_part(i)))] * 4
            + [pl.BlockSpec((stage_rows, gates.shape[1]), lambda i, p: (0, 0))]
            + whole_specs,
            scratch_shapes=[
                pltpu.VMEM((stage_rows, width), BRAIN),
                pltpu.VMEM((stage_rows, count * both_units), BRAIN),
                pltpu.SemaphoreType.DMA((4,)),
                pltpu.SemaphoreType.DMA,
            ],
        ),
        out_shape=[jax.ShapeDtypeStruct((rows, width), BRAIN)] * 4
        + [jax.ShapeDtypeStruct((stage_rows, gates.shape[1]), FLOAT)]
        + whole_shapes,
        input_output_aliases={9 + at: 5 + at for at in range(len(previous))},
        compiler_params=pltpu.CompilerParams(dimension_semantics=("arbitrary",)),
        cost_estimate=pl.CostEstimate(
            flops=4 * stage_rows * width * count * both_units,
            bytes_accessed=40 << 20,
            transcendentals=stage_rows * count * units,
        ),
        name="expert_stage",
    )(place, *blocks, down_back, gates, weights, weights_back, *previous)


def back_body(count, *refs):
    blocks = refs[: 4 * count]
    weights, rows_out, back_out, held, in_sems, out_sems = refs[4 * count :]
    step = pl.program_id(0)
    rows = blocks[0].shape[0]

    def incoming(slot):
        return [
            pltpu.make_async_copy(
                blocks[4 * slot + at],
                held.at[slot % 2, pl.ds(at * rows, rows), :],
                in_sems.at[slot % 2, at],
            )
            for at in range(4)
        ]

    def outgoing(slot):
        return [
            pltpu.make_async_copy(
                held.at[slot % 2, pl.ds(half * 2 * rows, 2 * rows), :],
                rows_out.at[pl.ds((half * count + slot) * 2 * rows, 2 * rows), :],
                out_sems.at[slot % 2, half],
            )
            for half in (0, 1)
        ]

    for slot in range(count):

        @pl.when(step == slot)
        def _(slot=slot):
            if slot == 0:
                for copy in incoming(0):
                    copy.start()
            if slot > 0:
                for copy in outgoing(slot - 1):
                    copy.wait()
            if slot + 1 < count:
                for copy in incoming(slot + 1):
                    copy.start()
            for copy in incoming(slot):
                copy.wait()
            for copy in outgoing(slot):
                copy.start()

    def one(at, carry):
        part = pl.ds(pl.multiple_of(at * rows, rows), rows)
        back_out[part, :] = jnp.dot(
            held[lax.rem(step, 2), part, :], weights[...], preferred_element_type=FLOAT
        ).astype(BRAIN)
        return carry

    lax.fori_loop(0, 4, one, 0)

    @pl.when(step == count - 1)
    def _():
        for copy in outgoing(count - 1):
            copy.wait()


def gathered_back(blocks, weights):
    rows, width = blocks[0].shape
    count = len(blocks) // 4
    units = weights.shape[1]
    anywhere = pl.BlockSpec(memory_space=pl.ANY)
    return pl.pallas_call(
        functools.partial(back_body, count),
        grid=(count,),
        in_specs=[anywhere] * len(blocks) + [pl.BlockSpec((width, units), lambda i: (0, 0))],
        out_specs=[anywhere, pl.BlockSpec((4 * rows, units), lambda i: (i, 0))],
        scratch_shapes=[
            pltpu.VMEM((2, 4 * rows, width), BRAIN),
            pltpu.SemaphoreType.DMA((2, 4)),
            pltpu.SemaphoreType.DMA((2, 2)),
        ],
        out_shape=[
            jax.ShapeDtypeStruct((4 * rows * count, width), BRAIN),
            jax.ShapeDtypeStruct((4 * rows * count, units), BRAIN),
        ],
        compiler_params=pltpu.CompilerParams(dimension_semantics=("arbitrary",)),
        cost_estimate=pl.CostEstimate(
            flops=8 * rows * count * width * units,
            bytes_accessed=48 << 20,
            transcendentals=0,
        ),
        name="gathered_back",
    )(*blocks, weights)


def placed_body(pairs, units, places, *refs):
    parts, outs = refs[:-2], refs[-2:]
    slots = len(parts) // 2
    for half in (0, 1):
        for slot in range(slots):
            lanes = pl.ds(pl.multiple_of(places[slot] * units, units), units)
            part = parts[half * slots + slot]
            for pair in range(pairs):
                for side in (0, 1):
                    first = (2 * pair + side) * units
                    outs[side][half * pairs + pair, :, lanes] = part[
                        :, first : first + units
                    ].astype(FLOAT)


def placed_grads(places, parts, local_experts, units):
    rows = parts[0].shape[0]
    slots = len(parts) // 2
    shape = (local_experts, rows, slots * units)
    return pl.pallas_call(
        functools.partial(placed_body, local_experts // 2, units),
        in_specs=[pl.BlockSpec(memory_space=pltpu.SMEM)]
        + [pl.BlockSpec(memory_space=pltpu.VMEM)] * len(parts),
        out_specs=[pl.BlockSpec(memory_space=pltpu.VMEM)] * 2,
        out_shape=[jax.ShapeDtypeStruct(shape, FLOAT)] * 2,
        cost_estimate=pl.CostEstimate(
            flops=8 * rows * slots * units, bytes_accessed=12 << 20, transcendentals=0
        ),
        name="placed_grads",
    )(places, *parts)


def swap_over(values, axis, bit):
    count = lax.axis_size(axis)
    return lax.ppermute(values, axis, [(at, at ^ bit) for at in range(count)])


def shift_over(values, axis, steps):
    count = lax.axis_size(axis)
    return lax.ppermute(values, axis, [(at, (at + steps) % count) for at in range(count)])


def axis_bits(axis):
    count = lax.axis_size(axis)
    return [1 << at for at in reversed(range(count.bit_length() - 1))]


def line_shards(
    tokens,
    routes,
    w_query,
    w_key,
    w_value,
    w_out,
    attn_gain,
    query_gain,
    key_gain,
    mlp_gain,
    router,
    w_gate,
    w_up,
    w_down,
    cotangent,
):
    inputs = tokens[0].astype(FLOAT)
    rows, width = inputs.shape
    ctx_count = lax.axis_size(CTX)
    dp_count = lax.axis_size(DP)
    expert_devices = lax.axis_size(EXPERT)
    plane = (DP, EXPERT)
    device_count = ctx_count * dp_count * expert_devices
    local_experts, _, units_all = w_gate.shape
    experts_all = local_experts * expert_devices
    units = units_all // ctx_count
    hidden_units = local_experts * units
    length = rows * ctx_count
    heads = HEADS // ctx_count
    columns = heads * HEAD_DIM
    score_scale = HEAD_DIM ** (-0.5)
    ctx_at = lax.axis_index(CTX)
    dp_at = lax.axis_index(DP)
    expert_at = lax.axis_index(EXPERT)
    first_column = ctx_at * columns
    ring_places = [(ctx_at + ctx_count - slot) % ctx_count for slot in range(ctx_count)]

    attn_inverse = norm_inverse(inputs)
    attn_in = (inputs * attn_inverse * attn_gain).astype(BRAIN)
    all_in = lax.all_gather(attn_in, CTX, axis=0, tiled=True)
    inverses = jnp.concatenate(
        [norm_inverse(times(attn_in, w_query)), norm_inverse(times(attn_in, w_key))], axis=1
    )
    all_inverses = lax.all_gather(inverses, CTX, axis=0, tiled=True)
    query_inverse = all_inverses[:, 0:1]
    key_inverse = all_inverses[:, 1:2]

    qkv_weights = jnp.concatenate(
        [
            lax.dynamic_slice_in_dim(weights, first_column, columns, axis=1)
            for weights in (w_query, w_key, w_value)
        ],
        axis=1,
    )
    query_gain_own = lax.dynamic_slice_in_dim(query_gain, first_column, columns, axis=0)
    key_gain_own = lax.dynamic_slice_in_dim(key_gain, first_column, columns, axis=0)
    cosine, sine_table = rope_tables(jnp.arange(length, dtype=jnp.int32))
    gate_slice, up_slice = [
        lax.dynamic_slice_in_dim(weights, ctx_at * units, units, axis=2)
        for weights in (w_gate, w_up)
    ]
    gate_up_weights = jnp.concatenate([gate_slice, up_slice], axis=2)
    gate_up_back = gate_up_weights.transpose(0, 2, 1).reshape(2 * hidden_units, width)
    down_weights = lax.dynamic_slice_in_dim(w_down, ctx_at * units, units, axis=1).reshape(
        hidden_units, width
    )

    down_across = down_weights.T
    all_in, upstream_low, gate_up_weights, gate_up_back, down_weights, down_across, qkv_weights = (
        meet(
            all_in,
            cotangent[0],
            gate_up_weights,
            gate_up_back,
            down_weights,
            down_across,
            qkv_weights,
        )
    )
    upstream = upstream_low.astype(FLOAT)
    near, far = axis_bits(EXPERT)[::-1]
    up_own = [upstream_low]
    up_own.append(shift_over(up_own[0], CTX, 1))
    up_far = [swap_over(up_own[0], EXPERT, far)]

    qkv_lin = times(all_in, qkv_weights)
    query_lin = qkv_lin[:, :columns]
    key_lin = qkv_lin[:, columns : 2 * columns]
    value_heads = qkv_lin[:, 2 * columns :].astype(BRAIN).reshape(length, heads, HEAD_DIM)
    query_heads = rotated(
        (query_lin * query_inverse * query_gain_own).reshape(length, heads, HEAD_DIM),
        cosine,
        sine_table,
    ).astype(BRAIN)
    key_heads = rotated(
        (key_lin * key_inverse * key_gain_own).reshape(length, heads, HEAD_DIM), cosine, sine_table
    ).astype(BRAIN)
    query_heads, key_heads, up_own[1], up_far[0] = meet(
        query_heads, key_heads, up_own[1], up_far[0]
    )
    up_own.append(shift_over(up_own[1], CTX, 1))
    up_far.append(swap_over(up_own[1], EXPERT, far))
    up_near = [swap_over(up_own[0], EXPERT, near)]
    up_both = [swap_over(up_far[0], EXPERT, near)]
    positions = jnp.arange(length, dtype=jnp.int32)
    visible = (positions[None, :] <= positions[:, None])[None]
    scores = (
        jnp.einsum("qhd,khd->hqk", query_heads, key_heads, preferred_element_type=FLOAT)
        * score_scale
    )
    scores = jnp.where(visible, scores, -1e30)
    probs = jax.nn.softmax(scores, axis=-1)
    probs_low = probs.astype(BRAIN)
    attn_wide = jnp.einsum("hqk,khd->qhd", probs_low, value_heads, preferred_element_type=FLOAT)
    attn_own = attn_wide.astype(BRAIN).reshape(length, columns)
    attn_own, up_own, up_far, up_near, up_both = meet(attn_own, up_own, up_far, up_near, up_both)
    up_far.append(swap_over(up_own[2], EXPERT, far))
    up_near.append(swap_over(up_own[1], EXPERT, near))
    up_near.append(swap_over(up_own[2], EXPERT, near))
    up_both.append(swap_over(up_far[1], EXPERT, near))
    attn_rows = lax.all_to_all(attn_own, CTX, split_axis=0, concat_axis=1, tiled=True)
    attn_rows, up_own, up_far, up_near, up_both = meet(
        attn_rows, up_own, up_far, up_near, up_both
    )
    up_own.append(shift_over(up_own[2], CTX, 1))
    up_both.append(swap_over(up_far[2], EXPERT, near))
    up_far.append(swap_over(up_own[3], EXPERT, far))
    up_near.append(swap_over(up_own[3], EXPERT, near))
    hidden = inputs + times(attn_rows, w_out)
    mlp_inverse = norm_inverse(hidden)
    expert_in = (hidden * mlp_inverse * mlp_gain).astype(BRAIN)
    logits = times(expert_in, router)
    gate_probs = jax.nn.softmax(logits, axis=-1)
    chosen = jnp.any(
        routes[0][:, :, None] == jnp.arange(experts_all, dtype=jnp.int32)[None, None, :], axis=1
    )
    gates = jnp.where(chosen, gate_probs, 0.0).astype(BRAIN)

    def dp_parts(partial, outer, inner):
        halves = partial.reshape(outer, dp_count, inner, -1)
        return (
            lax.dynamic_index_in_dim(halves, dp_at, axis=1, keepdims=False),
            swap_over(
                lax.dynamic_index_in_dim(halves, 1 - dp_at, axis=1, keepdims=False), DP, 1
            ),
        )

    def ctx_parts(blocks):
        return [
            shift_over(
                lax.dynamic_index_in_dim(
                    blocks, (ctx_at + at) % ctx_count, axis=0, keepdims=False
                ),
                CTX,
                at,
            )
            if at
            else lax.dynamic_index_in_dim(blocks, ctx_at, axis=0, keepdims=False)
            for at in range(ctx_count)
        ]

    grad_rows = width // (ctx_count * dp_count)
    padded_gates = jnp.pad(gates, ((0, 0), (0, -experts_all % 128)))
    first_expert = expert_at * local_experts
    expert_place = jnp.full((1,), first_expert, jnp.int32)

    moved_own = [expert_in]
    moved_far, moved_near, moved_both = [], [], []
    gate_slots, stages, near_sums, far_sums, half_grads = [], [], [], [], []
    buffers = produced = sent = total = gate_parts = None
    gate_half = padded_gates
    for tick in range(ctx_count + 5):
        slot = tick - 2
        fresh = {}
        if tick + 1 < ctx_count:
            fresh[OWN] = shift_over(moved_own[tick], CTX, 1)
        if tick < ctx_count:
            fresh[FAR] = swap_over(moved_own[tick], EXPERT, far)
            fresh[NEAR] = swap_over(moved_own[tick], EXPERT, near)
        if 0 <= tick - 1 < ctx_count:
            fresh[BOTH] = swap_over(moved_far[tick - 1], EXPERT, near)
        if tick == 0:
            fresh[GATES] = jnp.concatenate([gate_half, swap_over(gate_half, EXPERT, far)])
            fresh[UP_BOTH] = swap_over(up_far[3], EXPERT, near)
        if tick == 1:
            fresh[GATES] = jnp.concatenate([gate_half, swap_over(gate_half, EXPERT, near)])
            fresh[BACK] = gathered_back(
                [
                    kind[at]
                    for at in range(ctx_count)
                    for kind in (up_own, up_far, up_near, up_both)
                ],
                down_across,
            )
        if 2 <= tick < ctx_count + 1:
            fresh[GATES] = shift_over(gate_slots[-1], CTX, 1)
        if 0 <= slot < ctx_count:
            fresh[STAGE] = expert_stage(
                slot,
                expert_place,
                (moved_own[slot], moved_far[slot], moved_near[slot], moved_both[slot]),
                down_back,
                gate_slots[slot],
                gate_up_weights,
                gate_up_back,
                buffers,
            )
        if 0 <= slot - 1 < ctx_count:
            grads = stages[slot - 1]
            fresh[NEAR_SUM] = (
                grads[0] + swap_over(grads[2], EXPERT, near),
                grads[1] + swap_over(grads[3], EXPERT, near),
            )
        if 0 <= slot - 2 < ctx_count:
            pair = near_sums[slot - 2]
            fresh[FAR_SUM] = pair[0] + swap_over(pair[1], EXPERT, far)
        if tick == ctx_count + 2:
            total = far_sums[1]
            all_rows, all_pre_grads, all_weighted = buffers
            fresh[MADE] = [times(all_weighted[half], down_weights).astype(BRAIN) for half in (0, 1)]
            gate_parts = jnp.stack([stage[4] for stage in stages]).astype(BRAIN)
            fresh[DGATE] = gate_parts[:, : 2 * rows] + swap_over(
                gate_parts[:, 2 * rows :], EXPERT, near
            )
        if tick >= ctx_count + 2:
            fresh[RING] = shift_over(total, CTX, 1)
        if tick == ctx_count + 3:
            taken = swap_over(produced[1], EXPERT, near)
            fresh[MADE] = [
                [
                    produced[0][place : place + rows] + taken[place : place + rows]
                    for place in (2 * at * rows, (2 * at + 1) * rows)
                ]
                for at in range(ctx_count)
            ]
            fresh[DGATE] = gate_parts[:, :rows] + swap_over(gate_parts[:, rows:], EXPERT, far)
        if tick == ctx_count + 4:
            fresh[DGATE] = sum(
                (
                    shift_over(gate_parts[at], CTX, ctx_count - at).astype(FLOAT)
                    for at in range(1, ctx_count)
                ),
                gate_parts[0].astype(FLOAT),
            )
            fresh[MADE] = [produced[1][0] + swap_over(produced[1][1], EXPERT, far), produced]
            first_parts = dp_parts(half_grads[0], ctx_count, grad_rows)
        if tick >= ctx_count + 3:
            half = tick - ctx_count - 3
            fresh[HALF] = outer_sum(
                all_rows, all_pre_grads[:, half * hidden_units :][:, :hidden_units]
            ).astype(BRAIN)
        fresh = meet(fresh)[0]
        if OWN in fresh:
            moved_own.append(fresh[OWN])
        if FAR in fresh:
            moved_far.append(fresh[FAR])
            moved_near.append(fresh[NEAR])
        if BOTH in fresh:
            moved_both.append(fresh[BOTH])
        if tick == 0:
            up_both.append(fresh[UP_BOTH])
            gate_half = fresh[GATES]
        elif GATES in fresh:
            gate_slots.append(fresh[GATES])
        if BACK in fresh:
            all_upstream, down_back = fresh[BACK]
        if STAGE in fresh:
            stages.append(fresh[STAGE][:5])
            buffers = fresh[STAGE][5:]
        if NEAR_SUM in fresh:
            near_sums.append(fresh[NEAR_SUM])
        if FAR_SUM in fresh:
            far_sums.append(fresh[FAR_SUM])
        if RING in fresh:
            following = far_sums[(tick - ctx_count) % ctx_count]
            total = fresh[RING] + following
        if DGATE in fresh:
            gate_parts = fresh[DGATE]
        if MADE in fresh:
            produced = fresh[MADE]
        if HALF in fresh:
            half_grads.append(fresh[HALF])
    expert_in_grad = total.astype(FLOAT)
    gate_grads = gate_parts[:, :experts_all]
    produced_total, produced = produced

    prob_grads = jnp.where(chosen, gate_grads, 0.0)
    logit_grads = (
        gate_probs * (prob_grads - jnp.sum(prob_grads * gate_probs, axis=-1, keepdims=True))
    ).astype(BRAIN)
    router_grad = outer_sum(expert_in, logit_grads)
    expert_in_grad = expert_in_grad + times_transpose(logit_grads, router)
    hidden_part, mlp_gain_grad = norm_backward(hidden, mlp_inverse, mlp_gain, expert_in_grad)
    hidden_grad = upstream + hidden_part
    hidden_low = hidden_grad.astype(BRAIN)
    attn_grad_rows = times_transpose(hidden_low, w_out).astype(BRAIN)
    second_parts = dp_parts(half_grads[1], ctx_count, grad_rows)
    produced_two = produced[2][0] + swap_over(produced[2][1], EXPERT, far)
    produced_three = produced[3][0] + swap_over(produced[3][1], EXPERT, far)
    produced_total = shift_over(produced_total, CTX, 1)
    attn_grad_rows, first_parts = meet(attn_grad_rows, first_parts)
    attn_grad = lax.all_to_all(
        attn_grad_rows.reshape(rows, ctx_count, columns).transpose(1, 0, 2),
        CTX,
        split_axis=0,
        concat_axis=0,
        tiled=True,
    ).reshape(length, columns)
    first_half = ctx_parts(first_parts[0] + first_parts[1])
    down_half = outer_sum(
        all_weighted.reshape(all_upstream.shape[0], hidden_units), all_upstream
    ).astype(BRAIN)
    attn_grad, produced_two, produced_three, down_half, produced, hidden_low, produced_total = meet(
        attn_grad, produced_two, produced_three, down_half, produced, hidden_low, produced_total
    )
    attn_grad_heads = attn_grad.reshape(length, heads, HEAD_DIM)
    out_weight_grad = outer_sum(attn_rows, hidden_low).astype(BRAIN)
    out_weight_grad = lax.psum_scatter(
        out_weight_grad.reshape(ctx_count, width // ctx_count, width),
        plane,
        scatter_dimension=1,
        tiled=True,
    )
    produced_zero = produced[0][0] + swap_over(produced[0][1], EXPERT, far)
    produced_total = shift_over(produced_total + produced_two, CTX, 1)
    row_delta = jnp.sum(attn_wide * attn_grad_heads.astype(FLOAT), axis=-1).T
    prob_grad = jnp.einsum(
        "qhd,khd->hqk", attn_grad_heads, value_heads, preferred_element_type=FLOAT
    )
    score_grad = (probs * (prob_grad - row_delta[..., None])).astype(BRAIN)
    score_grad, produced_total, second_parts = meet(score_grad, produced_total, second_parts)
    produced_total = shift_over(produced_total + produced_three, CTX, 1)
    second_half = ctx_parts(second_parts[0] + second_parts[1])
    down_parts = dp_parts(down_half, local_experts, units // dp_count)
    query_grad = (
        jnp.einsum("hqk,khd->qhd", score_grad, key_heads, preferred_element_type=FLOAT)
        * score_scale
    )
    key_grad = (
        jnp.einsum("hqk,qhd->khd", score_grad, query_heads, preferred_element_type=FLOAT)
        * score_scale
    )
    value_low = (
        jnp.einsum("hqk,qhd->khd", probs_low, attn_grad_heads, preferred_element_type=FLOAT)
        .astype(BRAIN)
        .reshape(length, columns)
    )
    query_grad, key_grad, value_low = meet(query_grad, key_grad, value_low)
    query_rot_grad = rotated_back(query_grad, cosine, sine_table).reshape(length, columns)
    key_rot_grad = rotated_back(key_grad, cosine, sine_table).reshape(length, columns)
    query_weighted = query_rot_grad * query_gain_own
    key_weighted = key_rot_grad * key_gain_own
    dots = jnp.stack(
        [jnp.sum(query_weighted * query_lin, axis=-1), jnp.sum(key_weighted * key_lin, axis=-1)]
    )
    dots = lax.psum(dots, CTX) * (1.0 / width)
    query_gain_grad = jnp.sum(query_rot_grad * query_lin * query_inverse, axis=0)
    key_gain_grad = jnp.sum(key_rot_grad * key_lin * key_inverse, axis=0)
    query_low = (
        query_inverse * query_weighted
        - query_lin * (query_inverse * query_inverse * query_inverse * dots[0][:, None])
    ).astype(BRAIN)
    key_low = (
        key_inverse * key_weighted
        - key_lin * (key_inverse * key_inverse * key_inverse * dots[1][:, None])
    ).astype(BRAIN)
    qkv_low = jnp.concatenate([query_low, key_low, value_low], axis=1)
    qkv_low, produced_total, out_weight_grad, first_half, second_half, down_parts, produced_zero = (
        meet(
            qkv_low,
            produced_total,
            out_weight_grad,
            first_half,
            second_half,
            down_parts,
            produced_zero,
        )
    )
    produced_total = produced_total + produced_zero
    mixed = hidden + produced_total.astype(FLOAT)
    down_weight_grad = (down_parts[0] + down_parts[1]).astype(FLOAT)
    out_weight_grad = sum(
        (
            part.astype(FLOAT)
            for part in ctx_parts(out_weight_grad)
        ),
        jnp.zeros(out_weight_grad.shape[1:], FLOAT),
    )

    attn_in_parts = times_transpose(qkv_low, qkv_weights)
    attn_gain_grad = jnp.sum(attn_in_parts * all_in.astype(FLOAT), axis=0) / attn_gain
    attn_in_low = attn_in_parts.astype(BRAIN)
    attn_in_slots = [
        lax.dynamic_slice_in_dim(attn_in_low, place * rows, rows, axis=0) for place in ring_places
    ]
    attn_in_total = shift_over(attn_in_slots[1], CTX, 1)
    attn_in_total = attn_in_total + attn_in_slots[2]
    attn_in_total = shift_over(attn_in_total, CTX, 1) + attn_in_slots[3]
    attn_in_grad = (shift_over(attn_in_total, CTX, 1) + attn_in_slots[0]).astype(FLOAT)
    gate_weight_grad, up_weight_grad = placed_grads(
        jnp.stack(ring_places).astype(jnp.int32), first_half + second_half, local_experts, units
    )

    empty = jnp.zeros((width,), FLOAT)
    small = jnp.concatenate(
        [
            jnp.stack(
                [
                    attn_gain_grad,
                    lax.dynamic_update_slice_in_dim(empty, query_gain_grad, first_column, axis=0),
                    lax.dynamic_update_slice_in_dim(empty, key_gain_grad, first_column, axis=0),
                    mlp_gain_grad,
                ],
                axis=0,
            ),
            router_grad.T,
        ],
        axis=0,
    )
    own_width = width // device_count
    small_count = 4 + experts_all
    small = small.reshape(small_count, device_count, own_width).transpose(1, 0, 2)
    small = small.reshape(ctx_count, dp_count, 2, 2, small_count * own_width // 128, 128)
    for axis, bit, mine, place in (
        (DP, 1, dp_at, 1),
        (EXPERT, far, expert_at // 2, 1),
        (EXPERT, near, expert_at % 2, 1),
    ):
        kept = lax.dynamic_index_in_dim(small, mine, axis=place, keepdims=False)
        given = lax.dynamic_index_in_dim(small, 1 - mine, axis=place, keepdims=False)
        small = kept + swap_over(given, axis, bit)
    qkv_weight_grad = outer_sum(all_in, qkv_low).astype(BRAIN)
    qkv_weight_grad = lax.psum_scatter(
        qkv_weight_grad.reshape(ctx_count, width // ctx_count, 3 * columns),
        plane,
        scatter_dimension=1,
        tiled=True,
    )
    qkv_weight_grad, small = meet(qkv_weight_grad, small)
    qkv_weight_grad = lax.all_to_all(qkv_weight_grad, CTX, split_axis=0, concat_axis=0, tiled=True)
    small = sum(ctx_parts(small)).reshape(small_count, own_width)
    qkv_weight_grad = (
        qkv_weight_grad.reshape(ctx_count, own_width, 3, columns)
        .transpose(2, 1, 0, 3)
        .reshape(3, own_width, width)
        .astype(FLOAT)
    )
    input_part, _ = norm_backward(inputs, attn_inverse, attn_gain, attn_in_grad)
    input_grad = hidden_grad + input_part

    return (
        mixed.astype(BRAIN)[None],
        input_grad[None],
        qkv_weight_grad[0],
        qkv_weight_grad[1],
        qkv_weight_grad[2],
        out_weight_grad,
        small[0],
        small[1],
        small[2],
        small[3],
        small[4:].T,
        gate_weight_grad,
        up_weight_grad,
        down_weight_grad,
    )


def solution(mesh):
    sizes = mesh.shape
    if not (sizes[CTX] == 4 and sizes[EXPERT] == 4 and sizes[DP] == 2):
        return placed_over(mesh, plane_shards)

    return placed_over(mesh, line_shards)


def placed_over(mesh, shards):
    return jax.shard_map(
        shards,
        mesh=mesh,
        in_specs=(
            P((DP, EXPERT), CTX, None),
            P((DP, EXPERT), CTX, None),
            P(),
            P(),
            P(),
            P(),
            P(),
            P(),
            P(),
            P(),
            P(),
            P(EXPERT, None, None),
            P(EXPERT, None, None),
            P(EXPERT, None, None),
            P((DP, EXPERT), CTX, None),
        ),
        out_specs=(
            P((DP, EXPERT), CTX, None),
            P((DP, EXPERT), CTX, None),
            P((CTX, DP, EXPERT), None),
            P((CTX, DP, EXPERT), None),
            P((CTX, DP, EXPERT), None),
            P((CTX, DP, EXPERT), None),
            P((CTX, DP, EXPERT)),
            P((CTX, DP, EXPERT)),
            P((CTX, DP, EXPERT)),
            P((CTX, DP, EXPERT)),
            P((CTX, DP, EXPERT), None),
            P(EXPERT, (CTX, DP), None),
            P(EXPERT, (CTX, DP), None),
            P(EXPERT, (CTX, DP), None),
        ),
        check_vma=False,
    )
```
